32 devices in a mesh: dp: 16 (over z, y, x), mp: 2 (over core).
Axes of the slice: x: 2, y: 2, z: 4, core: 2. Of those that a mesh axis runs over, the one named last changes fastest.
Arguments:
- tokens: bfloat16 [8192, 2048], P('dp'), may hold values from -6 to 6
- noise_cond: float32 [128, 8192], P('dp'), may hold values from -1.5 to 1.5
- slot_bucket: int32 [16], P('dp'), may hold values from 0 to 3, as said below
- image_height: int32 [16, 8], P('dp'), may hold values from 5 to 16, as said below
- image_width: int32 [16, 8], P('dp'), may hold values from 5 to 32, as said below
- weight_query: bfloat16 [2048, 2048], P('dp', 'mp'), may hold values from -0.1875 to 0.1875
- weight_key: bfloat16 [2048, 2048], P('dp', 'mp'), may hold values from -0.1875 to 0.1875
- weight_value: bfloat16 [2048, 2048], P('dp', 'mp'), may hold values from -0.125 to 0.125
- weight_out: bfloat16 [2048, 2048], P('mp', 'dp'), may hold values from -0.5 to 0.5
- weight_in: bfloat16 [2048, 8192], P('dp', 'mp'), may hold values from -0.125 to 0.125
- weight_back: bfloat16 [8192, 2048], P('mp', 'dp'), may hold values from -0.09375 to 0.09375
- cotangent: bfloat16 [8192, 2048], P('dp'), may hold values from -6 to 6
Outputs:
- block_output: bfloat16 [8192, 2048], P('dp')
- grad_tokens: float32 [8192, 2048], P('dp')
- grad_cond: float32 [128, 8192], P('dp')
- grad_query: float32 [2048, 2048], P('dp', 'mp')
- grad_key: float32 [2048, 2048], P('dp', 'mp')
- grad_value: float32 [2048, 2048], P('dp', 'mp')
- grad_out: float32 [2048, 2048], P('mp', 'dp')
- grad_in: float32 [2048, 8192], P('dp', 'mp')
- grad_back: float32 [8192, 2048], P('mp', 'dp')
The draws below stay inside these ranges and needn't reach their ends.
Inputs may be any that keep to these rules, and one draw needn't show every extreme that they name: `slot_bucket`: buckets 0 to 3 hold 8, 4, 2, 1 images of a slot; the first slot is of bucket 3. `image_height`: greater than half of the bucket's grid height and at most it: 8 for buckets 0 and 1, 16 for buckets 2 and 3; entries of images past the slot's count are unused. `image_width`: greater than half of the bucket's grid width and at most it: 8, 16, 16, 32 for buckets 0 to 3; entries of images past the slot's count are unused.
All inputs are finite; a program needn't handle non-finite values.
Results may differ from the reference program's by a relative error of at most 0.014.
Values may be sent and summed in bfloat16 or wider, within the bound.
No kernel may reach another device: no remote copies, remote signals or barrier semaphores. Data moves between devices by JAX's collectives and lax.ppermute only.
A program may use at most 384 MiB of HBM per device.

```python
import jax
import jax.numpy as jnp
from jax import lax

D = 2048
HEADS = 16
HD = 128
FF = 8192
GH = 16
GW = 32
IMG_SLOT = 8
SLOT = 512
SLOTS = 16
TOKENS = 8192
IMAGES = 128


def layout_draw(key):
    rolls = jax.random.randint(jax.random.fold_in(key, 7), (SLOTS,), 0, 6)
    first = jnp.arange(SLOTS, dtype=jnp.int32) == 0
    bucket = jnp.where(first, 3, jnp.minimum(rolls, 3)).astype(jnp.int32)
    choose = (bucket[:, None] == jnp.arange(4, dtype=jnp.int32)[None, :]).astype(jnp.int32)
    grid_h = jnp.sum(choose * jnp.array([GH // 2, GH // 2, GH, GH], jnp.int32)[None, :], axis=1)
    grid_w = jnp.sum(choose * jnp.array([GW // 4, GW // 2, GW // 2, GW], jnp.int32)[None, :], axis=1)
    tall_roll = jax.random.randint(jax.random.fold_in(key, 8), (SLOTS, IMG_SLOT), 0, 1 << 20)
    broad_roll = jax.random.randint(jax.random.fold_in(key, 9), (SLOTS, IMG_SLOT), 0, 1 << 20)
    tall = grid_h[:, None] - tall_roll % (grid_h[:, None] // 2)
    broad = grid_w[:, None] - broad_roll % (grid_w[:, None] // 2)
    leading = first[:, None] & (jnp.arange(IMG_SLOT, dtype=jnp.int32)[None, :] == 0)
    tall = jnp.where(leading, grid_h[:, None], tall).astype(jnp.int32)
    broad = jnp.where(leading, grid_w[:, None], broad).astype(jnp.int32)
    return (bucket, tall, broad)


def draw_slot_bucket(key, part):
    return layout_draw(key)[0]


def draw_image_height(key, part):
    return layout_draw(key)[1]


def draw_image_width(key, part):
    return layout_draw(key)[2]


def spiked(values, rng, source, target, shards_of, factor):
    owner, partner = [(jnp.arange(values.shape[axis_at]) // (values.shape[axis_at] // shards_of)).reshape([-1 if axis == axis_at else 1 for axis in range(values.ndim)]) for axis_at in (source, target)]
    chosen = jax.random.permutation(rng, shards_of)[partner]
    strong = (owner == chosen) | (owner == (partner + shards_of // 2) % shards_of)
    return jnp.where(strong, factor * values, values)


def shard_levels(key, shape, shards, low, top_value):
    gain = 1.0
    for dim, blocks in shards:
        draws = jax.random.uniform(jax.random.fold_in(jax.random.fold_in(key, 6), dim), (blocks,), jnp.float32, low / len(shards), top_value / len(shards))
        gain = gain * jnp.repeat(jnp.exp(draws), shape[dim] // blocks).reshape((-1,) + (1,) * (len(shape) - 1 - dim))
    return gain


def centred(own_key, extent, scale, bound, shards=(), held_as=jnp.bfloat16):
    entries = scale * jax.random.normal(own_key, extent, jnp.float32)
    if shards:
        entries = entries * shard_levels(own_key, extent, shards, -0.22, 0.18)
    return jnp.clip(entries, -bound, bound).astype(held_as)


def noise_with(own_key, extent, scale, most, split, heavy, kind=jnp.bfloat16):
    drawn = scale * jax.random.normal(own_key, extent, jnp.float32)
    if split:
        drawn = drawn * shard_levels(own_key, extent, split, -0.22, 0.18)
    return jnp.clip(spiked(drawn, jax.random.fold_in(own_key, 3), *heavy), -most, most).astype(kind)


def setup_inputs(seed: int = 0) -> dict:
    seeds = jax.random.split(jax.random.key(seed), 13)
    tokens = noise_with(seeds[0], (TOKENS, D), 1.0, 6.0, ((0, 16),), (0, 1, 16, 2.0))
    noise_cond = centred(seeds[1], (IMAGES, 4 * D), 0.25, 1.5, ((0, 16),), jnp.float32)
    slot_bucket = draw_slot_bucket(jax.random.fold_in(seeds[12], 71), 0)
    image_height = draw_image_height(jax.random.fold_in(seeds[12], 71), 0)
    image_width = draw_image_width(jax.random.fold_in(seeds[12], 71), 0)
    weight_query = centred(seeds[5], (D, D), (D // 2) ** -0.5, 0.1875, ((0, 16), (1, 2)))
    weight_key = centred(seeds[6], (D, D), (D // 2) ** -0.5, 0.1875, ((0, 16), (1, 2)))
    weight_value = centred(seeds[7], (D, D), D ** -0.5, 0.125, ((0, 16), (1, 2)))
    weight_out = centred(seeds[8], (D, D), (D // 16) ** -0.5, 0.5, ((0, 2), (1, 16)))
    weight_in = centred(seeds[9], (D, FF), D ** -0.5, 0.125, ((0, 16), (1, 2)))
    weight_back = centred(seeds[10], (FF, D), (FF // 2) ** -0.5, 0.09375, ((0, 2), (1, 16)))
    cotangent = noise_with(seeds[11], (TOKENS, D), 1.0, 6.0, ((0, 16),), (0, 1, 16, 2.0))
    return {"tokens": tokens, "noise_cond": noise_cond, "slot_bucket": slot_bucket, "image_height": image_height, "image_width": image_width, "weight_query": weight_query, "weight_key": weight_key, "weight_value": weight_value, "weight_out": weight_out, "weight_in": weight_in, "weight_back": weight_back, "cotangent": cotangent}


EPS = 1e-06
HIGH = lax.Precision.HIGHEST

@jax.custom_vjp
def low(v):
    return lax.optimization_barrier(v.astype(jnp.bfloat16)).astype(jnp.float32)

@jax.custom_vjp
def low_back(v):
    return v

def low_keep(v):
    return (low(v), None)

def low_pass(kept, grad):
    return (grad,)

def back_keep(v):
    return (v, None)

def back_low(kept, grad):
    return (low(grad),)
low.defvjp(low_keep, low_pass)
low_back.defvjp(back_keep, back_low)

def arrange(slot_bucket, image_height, image_width):
    places = jnp.arange(SLOT, dtype=jnp.int32)
    choose = (slot_bucket[:, None] == jnp.arange(4, dtype=jnp.int32)[None, :]).astype(jnp.int32)
    areas = lax.optimization_barrier(jnp.sum(choose * jnp.array([SLOT // 8, SLOT // 4, SLOT // 2, SLOT], jnp.int32)[None, :], axis=1))
    across = lax.optimization_barrier(jnp.sum(choose * jnp.array([GW // 4, GW // 2, GW // 2, GW], jnp.int32)[None, :], axis=1))
    image = places[None, :] // areas[:, None]
    inner = places[None, :] % areas[:, None]
    grid_row = inner // across[:, None]
    grid_col = inner % across[:, None]
    member = image[:, :, None] == jnp.arange(IMG_SLOT, dtype=jnp.int32)[None, None, :]
    tall = lax.optimization_barrier(jnp.sum(jnp.where(member, image_height[:, None, :], 0), axis=2))
    broad = lax.optimization_barrier(jnp.sum(jnp.where(member, image_width[:, None, :], 0), axis=2))
    real = (grid_row < tall) & (grid_col < broad)
    allowed = (image[:, :, None] == image[:, None, :]) & real[:, None, :]
    return (member.astype(jnp.float32), allowed)

def modulate(hidden, member, cond_part):
    mods = jnp.einsum('sti,sic->stc', member, cond_part, precision=HIGH)
    width = hidden.shape[-1]
    factor = lax.rsqrt(lax.optimization_barrier(jnp.mean(hidden * hidden, axis=-1, keepdims=True)) + EPS)
    return hidden * factor * (1.0 + mods[..., :width]) + mods[..., width:]

def attend(inputs):
    queries, keys_all, values, allowed = inputs
    scores = jnp.einsum('qhd,khd->hqk', queries, keys_all, precision=HIGH) * HD ** (-0.5)
    scores = low_back(scores)
    scores = jnp.where(allowed[None], scores, -1e+30)
    top = lax.optimization_barrier(jnp.max(scores, axis=-1, keepdims=True))
    weights = jnp.where(allowed[None], jnp.exp(scores - top), 0.0)
    probs = low(weights / lax.optimization_barrier(jnp.sum(weights, axis=-1, keepdims=True)))
    mixed = jnp.einsum('hqk,khd->qhd', probs, values, precision=HIGH)
    return mixed.reshape(SLOT, HEADS * HD)

def reference(tokens, noise_cond, slot_bucket, image_height, image_width, weight_query, weight_key, weight_value, weight_out, weight_in, weight_back, cotangent):
    member, allowed = arrange(slot_bucket, image_height, image_width)

    def forward(hidden, cond, w_query, w_key, w_value, w_out, w_in, w_back):
        hidden = hidden.reshape(SLOTS, SLOT, D)
        cond = cond.reshape(SLOTS, IMG_SLOT, 4 * D)
        first = low(modulate(hidden, member, cond[:, :, :2 * D])).reshape(SLOTS * SLOT, D)

        def project(weight):
            made = low(low_back(jnp.dot(first, weight, precision=HIGH)))
            return made.reshape(SLOTS, SLOT, HEADS, HD)
        attended = lax.map(jax.checkpoint(attend), (project(w_query), project(w_key), project(w_value), allowed))
        attended = low(low_back(attended.reshape(SLOTS * SLOT, D)))
        middle = hidden.reshape(SLOTS * SLOT, D) + low_back(jnp.dot(attended, w_out, precision=HIGH))
        second = low(modulate(middle.reshape(SLOTS, SLOT, D), member, cond[:, :, 2 * D:])).reshape(SLOTS * SLOT, D)
        before = low_back(jnp.dot(second, w_in, precision=HIGH))
        after = low(jax.nn.gelu(before, approximate=False))
        return middle + low_back(jnp.dot(after, w_back, precision=HIGH))
    primals = (tokens.astype(jnp.float32), noise_cond.astype(jnp.float32), weight_query.astype(jnp.float32), weight_key.astype(jnp.float32), weight_value.astype(jnp.float32), weight_out.astype(jnp.float32), weight_in.astype(jnp.float32), weight_back.astype(jnp.float32))
    result, pullback = jax.vjp(forward, *primals)
    grads = pullback(cotangent.astype(jnp.float32))
    return (result.astype(jnp.bfloat16), grads[0], grads[1], grads[2], grads[3], grads[4], grads[5], grads[6], grads[7])
```

```python
import jax
import jax.numpy as jnp
from jax import lax
from jax.sharding import Mesh, PartitionSpec as P

HD = 128
GW = 32
IMG_SLOT = 8
SLOT = 512
HALF = SLOT // 2
EPS = 1e-06
HIGH = lax.Precision.HIGHEST
BF = jnp.bfloat16
F32 = jnp.float32
PAIRED = (0, 4, 1, 6, 2, 5, 3, 7)
UNPAIRED = (0, 2, 4, 6, 1, 5, 3, 7)


def arrange(slot_bucket, image_height, image_width, places):
    choose = (slot_bucket[:, None] == jnp.arange(4, dtype=jnp.int32)[None, :]).astype(jnp.int32)
    areas = jnp.sum(
        choose * jnp.array([SLOT // 8, SLOT // 4, SLOT // 2, SLOT], jnp.int32)[None, :], axis=1
    )
    across = jnp.sum(
        choose * jnp.array([GW // 4, GW // 2, GW // 2, GW], jnp.int32)[None, :], axis=1
    )
    image = places[None, :] // areas[:, None]
    inner = places[None, :] % areas[:, None]
    grid_row = inner // across[:, None]
    grid_col = inner % across[:, None]
    member = image[:, :, None] == jnp.arange(IMG_SLOT, dtype=jnp.int32)[None, None, :]
    tall = jnp.sum(jnp.where(member, image_height[:, None, :], 0), axis=2)
    broad = jnp.sum(jnp.where(member, image_width[:, None, :], 0), axis=2)
    real = (grid_row < tall) & (grid_col < broad)
    return image, real


def modulate(hidden, member, cond_part):
    width = hidden.shape[-1]
    mods = jnp.einsum("ti,ic->tc", member, cond_part, precision=HIGH)
    factor = lax.rsqrt(jnp.mean(hidden * hidden, axis=-1, keepdims=True) + EPS)
    return hidden * factor * (1.0 + mods[:, :width]) + mods[:, width:]


def contract_rows(left, right):
    return lax.dot_general(left, right, (((0,), (0,)), ((), ())), preferred_element_type=F32)


def times_transposed(left, right):
    return lax.dot_general(left, right, (((1,), (1,)), ((), ())), preferred_element_type=F32)


def times(left, right):
    return jnp.dot(left, right, preferred_element_type=F32)


def reorder(rows, order):
    blocks = rows.reshape(8, HALF, rows.shape[-1])
    return jnp.concatenate([blocks[i] for i in order], axis=0)


def heads_of(rows):
    return rows.reshape(4, SLOT, -1, HD)


def attend_forward(queries, keys_low, values, allowed):
    scores = jnp.einsum(
        "sqhd,skhd->shqk", queries, keys_low, preferred_element_type=F32
    ) * HD ** (-0.5)
    scores = jnp.where(allowed, scores, -1e30)
    top = jnp.max(scores, axis=-1, keepdims=True)
    weights = jnp.where(allowed, jnp.exp(scores - top), 0.0)
    total = jnp.sum(weights, axis=-1, keepdims=True)
    probs = (weights / total).astype(BF)
    mixed = jnp.einsum("shqk,skhd->sqhd", probs, values, preferred_element_type=F32)
    return mixed.astype(BF).reshape(4 * SLOT, -1), top + jnp.log(total)


def attend_backward(queries, keys_low, values, allowed, logsum, grad_mixed):
    scale = HD ** (-0.5)
    scores = jnp.einsum("sqhd,skhd->shqk", queries, keys_low, preferred_element_type=F32) * scale
    probs = jnp.where(allowed, jnp.exp(scores - logsum), 0.0)
    grad_values = jnp.einsum(
        "shqk,sqhd->skhd", probs.astype(BF), grad_mixed, preferred_element_type=F32
    )
    grad_probs = jnp.einsum("sqhd,skhd->shqk", grad_mixed, values, preferred_element_type=F32)
    grad_scores = probs * (grad_probs - jnp.sum(probs * grad_probs, axis=-1, keepdims=True))
    grad_scores = grad_scores.astype(BF)
    grad_queries = (
        jnp.einsum("shqk,skhd->sqhd", grad_scores, keys_low, preferred_element_type=F32) * scale
    )
    grad_keys = (
        jnp.einsum("shqk,sqhd->skhd", grad_scores, queries, preferred_element_type=F32) * scale
    )
    return tuple(
        part.astype(BF).reshape(4 * SLOT, -1) for part in (grad_queries, grad_keys, grad_values)
    )


def solution(mesh):
    outer = mesh.shape["dp"] // 4
    inner_mesh = Mesh(mesh.devices.reshape(outer, 2, 2, 2), ("o", "y", "x", "mp"))
    every = ("o", "y", "x", "mp")

    def pairs(move):
        made = []
        for o in range(outer):
            for y in range(2):
                for x in range(2):
                    for m in range(2):
                        ty, tx, tm = move(y, x, m)
                        made.append(
                            (((o * 2 + y) * 2 + x) * 2 + m, ((o * 2 + ty) * 2 + tx) * 2 + tm)
                        )
        return made

    near = pairs(lambda y, x, m: (y, 1 - x, m) if m == 0 else (1 - y, x, m))
    next_near = pairs(lambda y, x, m: (1 - y, x, m) if m == 0 else (y, 1 - x, m))
    sibling = pairs(lambda y, x, m: (y, x, 1 - m))
    offsets = {
        k: pairs(lambda y, x, m, k=k: (y ^ (k >> 1), x ^ (k & 1), m)) for k in (1, 2, 3)
    }

    def move(value, how):
        return lax.ppermute(value, every, how)

    def gather_rows(own):
        first = jnp.concatenate([own, move(own, near)], axis=0)
        second = move(first, next_near)
        return jnp.concatenate(
            [first, second, move(first, sibling), move(second, sibling)], axis=0
        )

    def scatter_rows(left, right):
        quarter = left.shape[0] // 4

        def part(i):
            return times_transposed(left[i * quarter : (i + 1) * quarter], right)

        far = part(1) + move(part(3).astype(BF), sibling).astype(F32)
        got = move(far.astype(BF), next_near)
        close = part(0) + move(part(2).astype(BF), sibling).astype(F32)
        close = close + got.astype(F32)
        return close[:HALF] + move(close[HALF:].astype(BF), near).astype(F32)

    def spread_weight(shard, blocks):
        rows = shard.shape[0]
        chip = lax.axis_index("y") * 2 + lax.axis_index("x")
        parts = shard.reshape(rows, blocks, 4, -1)
        width = parts.shape[-1]
        gathered = jnp.zeros((4, rows, blocks * width), shard.dtype)
        for k in range(4):
            there = chip ^ k
            piece = lax.dynamic_index_in_dim(parts, there, 2, keepdims=False)
            piece = piece.reshape(rows, blocks * width)
            if k:
                piece = move(piece, offsets[k])
            gathered = lax.dynamic_update_slice(gathered, piece[None], (there, 0, 0))
        gathered = gathered.reshape(4 * rows, blocks * width)
        return lax.all_gather(gathered, "o", axis=0, tiled=True)

    def collect_grad(partial, blocks):
        mine = lax.psum_scatter(partial, "o", scatter_dimension=0, tiled=True)
        chip = lax.axis_index("y") * 2 + lax.axis_index("x")
        rows = mine.shape[0] // 4
        width = mine.shape[1] // blocks
        mine = mine.reshape(4, rows, blocks, 1, width)
        result = jnp.zeros((rows, blocks, 4, width), F32)
        for k in range(4):
            there = chip ^ k
            piece = lax.dynamic_index_in_dim(mine, there, 0, keepdims=False)
            if k:
                piece = move(piece, offsets[k])
            result = lax.dynamic_update_slice(result, piece, (0, 0, there, 0))
        return result.reshape(rows, blocks, 4 * width)

    def local(
        tokens,
        noise_cond,
        slot_bucket,
        image_height,
        image_width,
        weight_query,
        weight_key,
        weight_value,
        weight_out,
        weight_in,
        weight_back,
        cotangent,
    ):
        core = lax.axis_index("mp")
        width = tokens.shape[1]
        places = (jnp.arange(SLOT, dtype=jnp.int32) + HALF * core) % SLOT
        facts = jnp.concatenate([slot_bucket[:, None], image_height, image_width], axis=1)
        facts = jnp.concatenate([facts, move(facts, near)], axis=0)
        facts = jnp.concatenate([facts, move(facts, next_near)], axis=0)
        image, real = arrange(
            facts[:, 0], facts[:, 1 : 1 + IMG_SLOT], facts[:, 1 + IMG_SLOT :], places
        )
        allowed = ((image[:, :, None] == image[:, None, :]) & real[:, None, :])[:, None]
        member = (
            image[0, :HALF, None] == jnp.arange(IMG_SLOT, dtype=jnp.int32)[None, :]
        ).astype(F32)
        first_cond = noise_cond[:, : 2 * width]
        second_cond = noise_cond[:, 2 * width :]

        qkv_full = spread_weight(
            jnp.concatenate([weight_query, weight_key, weight_value], axis=1), 3
        )
        out_full = spread_weight(weight_out.T, 1)
        in_full = spread_weight(weight_in, 1)
        back_full = spread_weight(weight_back.T, 1)

        hidden = lax.dynamic_slice(tokens, (core * HALF, 0), (HALF, width)).astype(F32)
        grad_result = lax.dynamic_slice(cotangent, (core * HALF, 0), (HALF, width))
        first = gather_rows(modulate(hidden, member, first_cond).astype(BF))
        cotangents = gather_rows(grad_result)

        qkv = reorder(times(first, qkv_full).astype(BF), PAIRED)
        part = qkv.shape[1] // 3
        queries, keys_low, values = (
            heads_of(qkv[:, i * part : (i + 1) * part]) for i in range(3)
        )
        attended, logsum = attend_forward(queries, keys_low, values, allowed)
        attended = reorder(attended, UNPAIRED)
        middle = hidden + scatter_rows(attended, out_full)
        second = gather_rows(modulate(middle, member, second_cond).astype(BF))
        before = times(second, in_full)

        def gelu_exact(pre_act):
            return jax.nn.gelu(pre_act, approximate=False)

        after, gelu_pullback = jax.vjp(gelu_exact, before)
        after = after.astype(BF)
        grad_back = collect_grad(contract_rows(cotangents, after), 1)
        grad_before = gelu_pullback(times(cotangents, back_full))[0].astype(BF)
        grad_in = collect_grad(contract_rows(second, grad_before), 1)
        grad_second = scatter_rows(grad_before, in_full)
        result = (middle + scatter_rows(after, back_full)).astype(BF)

        def norm(rows_in, cond_in):
            return modulate(rows_in, member, cond_in)

        unused, second_pullback = jax.vjp(norm, middle, second_cond)
        grad_middle_norm, grad_second_cond = second_pullback(grad_second)
        grad_middle = grad_result.astype(F32) + grad_middle_norm
        grad_branch = gather_rows(grad_middle.astype(BF))
        grad_out = collect_grad(contract_rows(grad_branch, attended), 1)
        grad_attended = reorder(times(grad_branch, out_full).astype(BF), PAIRED)
        grad_qkv = attend_backward(
            queries, keys_low, values, allowed, logsum, heads_of(grad_attended)
        )
        grad_qkv = reorder(jnp.concatenate(grad_qkv, axis=1), UNPAIRED)
        grad_qkv_weight = collect_grad(contract_rows(first, grad_qkv), 3)
        grad_first = scatter_rows(grad_qkv, qkv_full)
        unused, first_pullback = jax.vjp(norm, hidden, first_cond)
        grad_hidden_norm, grad_first_cond = first_pullback(grad_first)
        grad_tokens = grad_middle + grad_hidden_norm
        grad_cond = jnp.concatenate([grad_first_cond, grad_second_cond], axis=1)
        grad_cond = grad_cond + move(grad_cond, sibling)

        def both_halves(rows):
            other = move(rows, sibling)
            made = jnp.zeros((SLOT, width), rows.dtype)
            made = lax.dynamic_update_slice(made, rows, (core * HALF, 0))
            return lax.dynamic_update_slice(made, other, ((1 - core) * HALF, 0))

        return (
            both_halves(result),
            both_halves(grad_tokens),
            grad_cond,
            grad_qkv_weight[:, 0],
            grad_qkv_weight[:, 1],
            grad_qkv_weight[:, 2],
            grad_out[:, 0].T,
            grad_in[:, 0],
            grad_back[:, 0].T,
        )

    dp = ("o", "y", "x")
    return jax.shard_map(
        local,
        mesh=inner_mesh,
        in_specs=(
            P(dp, None),
            P(dp, None),
            P(dp),
            P(dp, None),
            P(dp, None),
            P(dp, "mp"),
            P(dp, "mp"),
            P(dp, "mp"),
            P("mp", dp),
            P(dp, "mp"),
            P("mp", dp),
            P(dp, None),
        ),
        out_specs=(
            P(dp, None),
            P(dp, None),
            P(dp, None),
            P(dp, "mp"),
            P(dp, "mp"),
            P(dp, "mp"),
            P("mp", dp),
            P(dp, "mp"),
            P("mp", dp),
        ),
        check_vma=False,
    )
```

```python
import jax
import jax.numpy as jnp
from jax import lax
from jax.sharding import Mesh, PartitionSpec as P

HD = 128
GW = 32
IMG_SLOT = 8
SLOT = 512
HALF = SLOT // 2
EPS = 1e-06
HIGH = lax.Precision.HIGHEST
BF = jnp.bfloat16
F32 = jnp.float32
PAIRED = (0, 4, 1, 6, 2, 5, 3, 7)
UNPAIRED = (0, 2, 4, 6, 1, 5, 3, 7)


def arrange(slot_bucket, image_height, image_width, places):
    choose = (slot_bucket[:, None] == jnp.arange(4, dtype=jnp.int32)[None, :]).astype(jnp.int32)
    areas = jnp.sum(
        choose * jnp.array([SLOT // 8, SLOT // 4, SLOT // 2, SLOT], jnp.int32)[None, :], axis=1
    )
    across = jnp.sum(
        choose * jnp.array([GW // 4, GW // 2, GW // 2, GW], jnp.int32)[None, :], axis=1
    )
    image = places[None, :] // areas[:, None]
    inner = places[None, :] % areas[:, None]
    grid_row = inner // across[:, None]
    grid_col = inner % across[:, None]
    member = image[:, :, None] == jnp.arange(IMG_SLOT, dtype=jnp.int32)[None, None, :]
    tall = jnp.sum(jnp.where(member, image_height[:, None, :], 0), axis=2)
    broad = jnp.sum(jnp.where(member, image_width[:, None, :], 0), axis=2)
    real = (grid_row < tall) & (grid_col < broad)
    return image, real


def modulate(hidden, member, cond_part):
    width = hidden.shape[-1]
    mods = jnp.einsum("ti,ic->tc", member, cond_part, precision=HIGH)
    factor = lax.rsqrt(jnp.mean(hidden * hidden, axis=-1, keepdims=True) + EPS)
    return hidden * factor * (1.0 + mods[:, :width]) + mods[:, width:]


def contract_rows(left, right):
    return lax.dot_general(left, right, (((0,), (0,)), ((), ())), preferred_element_type=F32)


def times_transposed(left, right):
    return lax.dot_general(left, right, (((1,), (1,)), ((), ())), preferred_element_type=F32)


def times(left, right):
    return jnp.dot(left, right, preferred_element_type=F32)


def reorder(rows, order):
    blocks = rows.reshape(8, HALF, rows.shape[-1])
    return jnp.concatenate([blocks[i] for i in order], axis=0)


def heads_of(rows):
    return rows.reshape(4, SLOT, -1, HD)


def attend_forward(queries, keys_low, values, allowed):
    scores = jnp.einsum(
        "sqhd,skhd->shqk", queries, keys_low, preferred_element_type=F32
    ) * HD ** (-0.5)
    scores = jnp.where(allowed, scores, -1e30)
    top = jnp.max(scores, axis=-1, keepdims=True)
    weights = jnp.where(allowed, jnp.exp(scores - top), 0.0)
    total = jnp.sum(weights, axis=-1, keepdims=True)
    probs = (weights / total).astype(BF)
    mixed = jnp.einsum("shqk,skhd->sqhd", probs, values, preferred_element_type=F32)
    return mixed.astype(BF).reshape(4 * SLOT, -1), top + jnp.log(total)


def attend_backward(queries, keys_low, values, allowed, logsum, grad_mixed):
    scale = HD ** (-0.5)
    scores = jnp.einsum("sqhd,skhd->shqk", queries, keys_low, preferred_element_type=F32) * scale
    probs = jnp.where(allowed, jnp.exp(scores - logsum), 0.0)
    grad_values = jnp.einsum(
        "shqk,sqhd->skhd", probs.astype(BF), grad_mixed, preferred_element_type=F32
    )
    grad_probs = jnp.einsum("sqhd,skhd->shqk", grad_mixed, values, preferred_element_type=F32)
    grad_scores = probs * (grad_probs - jnp.sum(probs * grad_probs, axis=-1, keepdims=True))
    grad_scores = grad_scores.astype(BF)
    grad_queries = (
        jnp.einsum("shqk,skhd->sqhd", grad_scores, keys_low, preferred_element_type=F32) * scale
    )
    grad_keys = (
        jnp.einsum("shqk,sqhd->skhd", grad_scores, queries, preferred_element_type=F32) * scale
    )
    return tuple(
        part.astype(BF).reshape(4 * SLOT, -1) for part in (grad_queries, grad_keys, grad_values)
    )


def solution(mesh):
    outer = mesh.shape["dp"] // 4
    inner_mesh = Mesh(mesh.devices.reshape(outer, 2, 2, 2), ("o", "y", "x", "mp"))
    every = ("o", "y", "x", "mp")

    def pairs(move):
        made = []
        for o in range(outer):
            for y in range(2):
                for x in range(2):
                    for m in range(2):
                        ty, tx, tm = move(y, x, m)
                        made.append(
                            (((o * 2 + y) * 2 + x) * 2 + m, ((o * 2 + ty) * 2 + tx) * 2 + tm)
                        )
        return made

    near = pairs(lambda y, x, m: (y, 1 - x, m) if m == 0 else (1 - y, x, m))
    next_near = pairs(lambda y, x, m: (1 - y, x, m) if m == 0 else (y, 1 - x, m))
    sibling = pairs(lambda y, x, m: (y, x, 1 - m))
    offsets = {
        k: pairs(lambda y, x, m, k=k: (y ^ (k >> 1), x ^ (k & 1), m)) for k in (1, 2, 3)
    }

    def move(value, how):
        return lax.ppermute(value, every, how)

    def gather_rows(own):
        first = jnp.concatenate([own, move(own, near)], axis=0)
        second = move(first, next_near)
        return jnp.concatenate(
            [first, second, move(first, sibling), move(second, sibling)], axis=0
        )

    def scatter_rows(left, right):
        quarter = left.shape[0] // 4

        def part(i):
            return times_transposed(left[i * quarter : (i + 1) * quarter], right)

        far = part(1) + move(part(3).astype(BF), sibling).astype(F32)
        got = move(far.astype(BF), next_near)
        close = part(0) + move(part(2).astype(BF), sibling).astype(F32)
        close = close + got.astype(F32)
        return close[:HALF] + move(close[HALF:].astype(BF), near).astype(F32)

    def in_place_order(pieces):
        far_row = lax.axis_index("y") == 1
        far_col = lax.axis_index("x") == 1
        return [
            jnp.where(
                far_row,
                jnp.where(far_col, pieces[j ^ 3], pieces[j ^ 2]),
                jnp.where(far_col, pieces[j ^ 1], pieces[j]),
            )
            for j in range(4)
        ]

    def exchange(blocks_of):
        chip = lax.axis_index("y") * 2 + lax.axis_index("x")
        pieces = [blocks_of(chip)]
        for k in (1, 2, 3):
            pieces.append(move(blocks_of(chip ^ k), offsets[k]))
        return pieces

    def weight_pieces(shards):
        def blocks_of(chip):
            cut = []
            for shard in shards:
                part = shard.shape[1] // 4
                cut.append(lax.dynamic_slice_in_dim(shard, chip * part, part, 1))
            return jnp.concatenate(cut, axis=1)

        return exchange(blocks_of)

    def whole_plane(pieces, start, stop):
        return jnp.concatenate(in_place_order([p[:, start:stop] for p in pieces]), axis=0)

    def along(value):
        return lax.all_gather(value, "o", axis=0, tiled=True)

    def collect_grads(partials):
        summed = [lax.psum_scatter(p, "o", scatter_dimension=0, tiled=True) for p, _ in partials]
        made = []
        for i, (_, blocks) in enumerate(partials):
            mine = summed[i]
            rows = mine.shape[0] // 4
            width = mine.shape[1] // blocks
            pieces = exchange(lambda chip: lax.dynamic_slice_in_dim(mine, chip * rows, rows, 0))
            if i + 1 < len(partials):
                *pieces, summed[i + 1] = lax.optimization_barrier((*pieces, summed[i + 1]))
            made.append(
                [in_place_order([p[:, b * width : (b + 1) * width] for p in pieces])
                for b in range(blocks)]
            )
        return made

    def local(
        tokens,
        noise_cond,
        slot_bucket,
        image_height,
        image_width,
        weight_query,
        weight_key,
        weight_value,
        weight_out,
        weight_in,
        weight_back,
        cotangent,
    ):
        core = lax.axis_index("mp")
        width = tokens.shape[1]
        places = (jnp.arange(SLOT, dtype=jnp.int32) + HALF * core) % SLOT
        facts = jnp.concatenate([slot_bucket[:, None], image_height, image_width], axis=1)
        facts = jnp.concatenate([facts, move(facts, near)], axis=0)
        facts = jnp.concatenate([facts, move(facts, next_near)], axis=0)
        image, real = arrange(
            facts[:, 0], facts[:, 1 : 1 + IMG_SLOT], facts[:, 1 + IMG_SLOT :], places
        )
        allowed = ((image[:, :, None] == image[:, None, :]) & real[:, None, :])[:, None]
        member = (
            image[0, :HALF, None] == jnp.arange(IMG_SLOT, dtype=jnp.int32)[None, :]
        ).astype(F32)
        first_cond = noise_cond[:, : 2 * width]
        second_cond = noise_cond[:, 2 * width :]

        qkv_pieces = weight_pieces([weight_query, weight_key, weight_value])
        qkv_plane = whole_plane(qkv_pieces, 0, qkv_pieces[0].shape[1])
        qkv_full = along(qkv_plane)
        rest = weight_pieces([weight_out.T, weight_in, weight_back.T])
        head_width = weight_out.shape[0] // 4
        hidden_width = weight_in.shape[1] // 4
        out_full = along(whole_plane(rest, 0, head_width))
        in_full = along(whole_plane(rest, head_width, head_width + hidden_width))
        back_full = along(
            whole_plane(rest, head_width + hidden_width, head_width + 2 * hidden_width)
        )

        hidden = lax.dynamic_slice(tokens, (core * HALF, 0), (HALF, width)).astype(F32)
        grad_result = lax.dynamic_slice(cotangent, (core * HALF, 0), (HALF, width))
        first = gather_rows(modulate(hidden, member, first_cond).astype(BF))
        grad_result, first = lax.optimization_barrier((grad_result, first))
        cotangents = gather_rows(grad_result)

        qkv = reorder(times(first, qkv_full).astype(BF), PAIRED)
        part = qkv.shape[1] // 3
        queries, keys_low, values = (
            heads_of(qkv[:, i * part : (i + 1) * part]) for i in range(3)
        )
        attended, logsum = attend_forward(queries, keys_low, values, allowed)
        attended = reorder(attended, UNPAIRED)
        middle = hidden + scatter_rows(attended, out_full)
        second = gather_rows(modulate(middle, member, second_cond).astype(BF))
        before = times(second, in_full)

        def gelu_exact(pre_act):
            return jax.nn.gelu(pre_act, approximate=False)

        after, gelu_pullback = jax.vjp(gelu_exact, before)
        after = after.astype(BF)
        back_part = contract_rows(cotangents, after)
        back_part, cotangents = lax.optimization_barrier((back_part, cotangents))
        grad_before = gelu_pullback(times(cotangents, back_full))[0].astype(BF)
        in_part = contract_rows(second, grad_before)
        in_part, grad_before = lax.optimization_barrier((in_part, grad_before))
        grad_second = scatter_rows(grad_before, in_full)

        def norm(rows_in, cond_in):
            return modulate(rows_in, member, cond_in)

        unused, second_pullback = jax.vjp(norm, middle, second_cond)
        grad_middle_norm, grad_second_cond = second_pullback(grad_second)
        grad_middle = grad_result.astype(F32) + grad_middle_norm
        grad_branch = gather_rows(grad_middle.astype(BF))
        out_part = contract_rows(grad_branch, attended)
        out_part, grad_branch = lax.optimization_barrier((out_part, grad_branch))
        after, grad_branch = lax.optimization_barrier((after, grad_branch))
        grad_attended = reorder(times(grad_branch, out_full).astype(BF), PAIRED)
        grad_qkv = attend_backward(
            queries, keys_low, values, allowed, logsum, heads_of(grad_attended)
        )
        grad_qkv = reorder(jnp.concatenate(grad_qkv, axis=1), UNPAIRED)
        qkv_part = contract_rows(first, grad_qkv)
        qkv_part, grad_qkv = lax.optimization_barrier((qkv_part, grad_qkv))
        (grad_back,), (grad_in,), (grad_out,), grad_qkv_weight = collect_grads(
            [(back_part, 1), (in_part, 1), (out_part, 1), (qkv_part, 3)]
        )
        grad_first = scatter_rows(grad_qkv, qkv_full)
        result = (middle + scatter_rows(after, back_full)).astype(BF)
        unused, first_pullback = jax.vjp(norm, hidden, first_cond)
        grad_hidden_norm, grad_first_cond = first_pullback(grad_first)
        grad_tokens = grad_middle + grad_hidden_norm
        grad_cond = jnp.concatenate([grad_first_cond, grad_second_cond], axis=1)
        grad_cond = grad_cond + move(grad_cond, sibling)

        def both_halves(rows):
            other = move(rows, sibling)
            made = jnp.zeros((SLOT, width), rows.dtype)
            made = lax.dynamic_update_slice(made, rows, (core * HALF, 0))
            return lax.dynamic_update_slice(made, other, ((1 - core) * HALF, 0))

        return (
            both_halves(result),
            both_halves(grad_tokens),
            grad_cond,
            *[jnp.concatenate(part, axis=1) for part in grad_qkv_weight],
            jnp.concatenate([part.T for part in grad_out], axis=0),
            jnp.concatenate(grad_in, axis=1),
            jnp.concatenate([part.T for part in grad_back], axis=0),
        )

    dp = ("o", "y", "x")
    return jax.shard_map(
        local,
        mesh=inner_mesh,
        in_specs=(
            P(dp, None),
            P(dp, None),
            P(dp),
            P(dp, None),
            P(dp, None),
            P(dp, "mp"),
            P(dp, "mp"),
            P(dp, "mp"),
            P("mp", dp),
            P(dp, "mp"),
            P("mp", dp),
            P(dp, None),
        ),
        out_specs=(
            P(dp, None),
            P(dp, None),
            P(dp, None),
            P(dp, "mp"),
            P(dp, "mp"),
            P(dp, "mp"),
            P("mp", dp),
            P(dp, "mp"),
            P("mp", dp),
        ),
        check_vma=False,
    )
```

```python
import jax
import jax.numpy as jnp
from jax import lax
from jax.experimental import pallas as pl
from jax.experimental.pallas import tpu as pltpu
from jax.sharding import Mesh, PartitionSpec as P

HD = 128
GW = 32
IMG_SLOT = 8
SLOT = 512
HALF = SLOT // 2
EPS = 1e-06
HIGH = lax.Precision.HIGHEST
BF = jnp.bfloat16
F32 = jnp.float32


def arrange(slot_bucket, image_height, image_width, places):
    area_bits = 6 + slot_bucket[:, None]
    across_bits = 3 + ((slot_bucket[:, None] + 1) >> 1)
    image = places[None, :] >> area_bits
    inner = places[None, :] & ((1 << area_bits) - 1)
    grid_row = inner >> across_bits
    grid_col = inner & ((1 << across_bits) - 1)
    real = jnp.zeros(image.shape, bool)
    for i in range(IMG_SLOT):
        tall = image_height[:, i : i + 1]
        broad = image_width[:, i : i + 1]
        real = real | ((image == i) & (grid_row < tall) & (grid_col < broad))
    return image, real


def modulate(hidden, member, cond_part):
    width = hidden.shape[-1]
    mods = jnp.einsum("ti,ic->tc", member, cond_part, precision=HIGH)
    factor = lax.rsqrt(jnp.mean(hidden * hidden, axis=-1, keepdims=True) + EPS)
    return hidden * factor * (1.0 + mods[:, :width]) + mods[:, width:]


def nt(a,b): return lax.dot_general(a,b,(((1,),(1,)),((),())),preferred_element_type=F32)
def nn(a,b): return lax.dot_general(a,b,(((1,),(0,)),((),())),preferred_element_type=F32)
def tn(a,b): return lax.dot_general(a,b,(((0,),(0,)),((),())),preferred_element_type=F32)

def softmax_of(queries, keys_low, allowed):
    scores = nt(queries, keys_low) * HD ** (-0.5)
    scores = jnp.where(allowed, scores, -1e30)
    top = jnp.max(scores, axis=-1, keepdims=True)
    weights = jnp.where(allowed, jnp.exp(scores - top), 0.0)
    return weights / jnp.sum(weights, axis=-1, keepdims=True)

def column(block, i, j, heads):
    at = (i * heads + j) * HD
    return block[:, at : at + HD]

def mask_of(facts, of_key):
    places = lax.broadcasted_iota(jnp.int32, (SLOT, 1), 0) + facts[4]
    image = (places & (SLOT - 1)) >> facts[pl.program_id(0)]
    return image == of_key[0]

def attend_kernel(mine, sib, facts, of_key, out_mine, out_sib):
    allowed = mask_of(facts, of_key)
    rows = jnp.concatenate([mine[...], sib[...]], axis=0)
    heads = rows.shape[1] // (3 * HD)
    made = []
    for j in range(heads):
        probs = softmax_of(column(rows, 0, j, heads), column(rows, 1, j, heads), allowed)
        made.append(nn(probs.astype(BF), column(rows, 2, j, heads)).astype(BF))
    made = jnp.concatenate(made, axis=1)
    out_mine[...] = made[:HALF]
    out_sib[...] = made[HALF:]

def attend_back_kernel(mine, grad_mine, sib, grad_sib, facts, of_key, out_mine, out_sib):
    allowed = mask_of(facts, of_key)
    rows = jnp.concatenate([mine[...], sib[...]], axis=0)
    grads = jnp.concatenate([grad_mine[...], grad_sib[...]], axis=0)
    heads = rows.shape[1] // (3 * HD)
    scale = HD ** (-0.5)
    parts = [[], [], []]
    for j in range(heads):
        queries, keys_low, values = (column(rows, i, j, heads) for i in range(3))
        grad_mixed = column(grads, 0, j, heads)
        probs = softmax_of(queries, keys_low, allowed)
        grad_values = tn(probs.astype(BF), grad_mixed)
        grad_probs = nt(grad_mixed, values)
        grad_scores = probs * (grad_probs - jnp.sum(probs * grad_probs, axis=-1, keepdims=True))
        grad_scores = grad_scores.astype(BF)
        parts[0].append((nn(grad_scores, keys_low) * scale).astype(BF))
        parts[1].append((tn(grad_scores, queries) * scale).astype(BF))
        parts[2].append(grad_values.astype(BF))
    made = jnp.concatenate(parts[0] + parts[1] + parts[2], axis=1)
    out_mine[...] = made[:HALF]
    out_sib[...] = made[HALF:]

def at_mine(s): return (s, 0)
def at_sib(s): return ((s // 2) + (s % 2) * 2, 0)
def at_slot(s): return (s, 0, 0)

def attention(kernel, halves, facts, of_key, width):
    specs = []
    for i, rows in enumerate(halves):
        where = at_mine if i < len(halves) // 2 else at_sib
        specs.append(pl.BlockSpec((HALF, rows.shape[1]), where))
    specs.append(pl.BlockSpec(memory_space=pltpu.SMEM))
    specs.append(pl.BlockSpec((1, 1, SLOT), at_slot))
    made = jax.ShapeDtypeStruct((4 * HALF, width), BF)
    return pl.pallas_call(
        kernel,
        grid=(4,),
        in_specs=specs,
        out_specs=[pl.BlockSpec((HALF, width), at_mine), pl.BlockSpec((HALF, width), at_sib)],
        out_shape=[made, made],
    )(*halves, facts, of_key)

ERFC = (-1.26551223, 1.00002368, 0.37409196, 0.09678418, -0.18628806, 0.27886807,
        -1.13520398, 1.48851587, -0.82215223, 0.17087277)

def gelu_parts(u):
    z = jnp.abs(u) * 0.7071067811865476
    t = 1.0 / (1.0 + 0.5 * z)
    poly = jnp.full_like(t, ERFC[-1])
    for c in ERFC[-2::-1]:
        poly = poly * t + c
    bell = jnp.exp(-0.5 * u * u)
    tail = 0.5 * t * bell * jnp.exp(poly)
    phi = jnp.where(u < 0, tail, 1.0 - tail)
    return u * phi, phi + u * bell * 0.3989422804014327


def up_kernel(rows, weight, after, slope):
    made, rate = gelu_parts(nn(rows[...], weight[...]))
    after[...] = made.astype(BF)
    slope[...] = rate


def down_kernel(rows, weight, slope, grad):
    grad[...] = (nn(rows[...], weight[...]) * slope[...]).astype(BF)


def hidden_up(rows, weight, tile=256):
    count, depth = rows.shape
    width = weight.shape[1]
    by_row = lambda i: (i, 0)
    return pl.pallas_call(
        up_kernel,
        grid=(count // tile,),
        in_specs=[pl.BlockSpec((tile, depth), by_row), pl.BlockSpec((depth, width), lambda i: (0, 0))],
        out_specs=[pl.BlockSpec((tile, width), by_row), pl.BlockSpec((tile, width), by_row)],
        out_shape=[
            jax.ShapeDtypeStruct((count, width), BF),
            jax.ShapeDtypeStruct((count, width), F32),
        ],
    )(rows, weight)


def hidden_down(rows, weight, slope, tile=256):
    count, depth = rows.shape
    width = weight.shape[1]
    by_row = lambda i: (i, 0)
    return pl.pallas_call(
        down_kernel,
        grid=(count // tile,),
        in_specs=[
            pl.BlockSpec((tile, depth), by_row),
            pl.BlockSpec((depth, width), lambda i: (0, 0)),
            pl.BlockSpec((tile, width), by_row),
        ],
        out_specs=pl.BlockSpec((tile, width), by_row),
        out_shape=jax.ShapeDtypeStruct((count, width), BF),
    )(rows, weight, slope)


def grad_kernel(left_mine, right_mine, left_sib, right_sib, made):
    made[...] = tn(left_mine[...], right_mine[...]) + tn(left_sib[...], right_sib[...])


def weight_grad(left, right, tile=512):
    count, depth = left[0].shape
    width = right[0].shape[1]
    specs = [
        pl.BlockSpec((count, tile), lambda i: (0, i)),
        pl.BlockSpec((count, width), lambda i: (0, 0)),
    ]
    return pl.pallas_call(
        grad_kernel,
        grid=(depth // tile,),
        in_specs=specs + specs,
        out_specs=pl.BlockSpec((tile, width), lambda i: (i, 0)),
        out_shape=jax.ShapeDtypeStruct((depth, width), F32),
    )(left[0], right[0], left[1], right[1])


def solution(mesh):
    outer = mesh.shape["dp"] // 4
    inner_mesh = Mesh(mesh.devices.reshape(outer, 2, 2, 2), ("o", "y", "x", "mp"))
    every = ("o", "y", "x", "mp")

    def pairs(move):
        made = []
        for o in range(outer):
            for y in range(2):
                for x in range(2):
                    for m in range(2):
                        ty, tx, tm = move(y, x, m)
                        made.append(
                            (((o * 2 + y) * 2 + x) * 2 + m, ((o * 2 + ty) * 2 + tx) * 2 + tm)
                        )
        return made

    near = pairs(lambda y, x, m: (y, 1 - x, m) if m == 0 else (1 - y, x, m))
    next_near = pairs(lambda y, x, m: (1 - y, x, m) if m == 0 else (y, 1 - x, m))
    sibling = pairs(lambda y, x, m: (y, x, 1 - m))
    offsets = {
        k: pairs(lambda y, x, m, k=k: (y ^ (k >> 1), x ^ (k & 1), m)) for k in (1, 2, 3)
    }

    def move(value, how):
        return lax.ppermute(value, every, how)

    def gather_rows(own):
        return gather_further(jnp.concatenate([own, move(own, near)], axis=0))

    def gather_further(first):
        mine = jnp.concatenate([first, move(first, next_near)], axis=0)
        return mine, move(mine, sibling)

    def scatter_rows(left, right):
        mine, sib = left
        middle = mine.shape[0] // 2
        far = nt(mine[middle:], right)
        far = far + move(nt(sib[middle:], right).astype(BF), sibling).astype(F32)
        got = move(far.astype(BF), next_near)
        close = nt(mine[:middle], right)
        close = close + move(nt(sib[:middle], right).astype(BF), sibling).astype(F32)
        close = close + got.astype(F32)
        return close[:HALF] + move(close[HALF:].astype(BF), near).astype(F32)

    def in_place_order(pieces):
        far_row = lax.axis_index("y") == 1
        far_col = lax.axis_index("x") == 1
        return [
            jnp.where(
                far_row,
                jnp.where(far_col, pieces[j ^ 3], pieces[j ^ 2]),
                jnp.where(far_col, pieces[j ^ 1], pieces[j]),
            )
            for j in range(4)
        ]

    def exchange(blocks_of):
        chip = lax.axis_index("y") * 2 + lax.axis_index("x")
        pieces = [blocks_of(chip)]
        for k in (1, 2, 3):
            pieces.append(move(blocks_of(chip ^ k), offsets[k]))
        return pieces

    def weight_pieces(shards):
        rows = shards[0].shape[0]
        stack = []
        for c in range(4):
            cut = [shard[:, c * (n // 4) : (c + 1) * (n // 4)] for shard in shards for n in (shard.shape[1],)]
            stack.append(jnp.concatenate(cut, axis=1))
        stack = lax.optimization_barrier(jnp.concatenate(stack, axis=0))
        return exchange(lambda chip: lax.dynamic_slice_in_dim(stack, chip * rows, rows, 0))

    def whole_plane(pieces, start, stop):
        return jnp.concatenate(in_place_order([p[:, start:stop] for p in pieces]), axis=0)

    def along(value):
        return lax.all_gather(value, "o", axis=0, tiled=True)

    def along_sum(value):
        return lax.psum_scatter(value, "o", scatter_dimension=0, tiled=True)

    def after_sum(mine):
        rows = mine.shape[0] // 4
        return exchange(lambda chip: lax.dynamic_slice_in_dim(mine, chip * rows, rows, 0))

    def before_sum(partial):
        parts = partial.reshape(outer, 4, partial.shape[0] // (4 * outer), -1)

        def blocks_of(chip):
            cut = lax.dynamic_slice_in_dim(parts, chip, 1, 1)
            return cut.reshape(-1, partial.shape[1])

        return exchange(blocks_of)

    def local(
        tokens,
        noise_cond,
        slot_bucket,
        image_height,
        image_width,
        weight_query,
        weight_key,
        weight_value,
        weight_out,
        weight_in,
        weight_back,
        cotangent,
    ):
        core = lax.axis_index("mp")
        width = tokens.shape[1]
        places = (jnp.arange(SLOT, dtype=jnp.int32) + HALF * core) % SLOT
        facts = jnp.concatenate([slot_bucket[:, None], image_height, image_width], axis=1)
        facts = jnp.concatenate([facts, move(facts, near)], axis=0)
        facts = jnp.concatenate([facts, move(facts, next_near)], axis=0)
        image, real = arrange(
            facts[:, 0], facts[:, 1 : 1 + IMG_SLOT], facts[:, 1 + IMG_SLOT :], places
        )
        slot_facts = jnp.concatenate([6 + facts[:, 0], HALF * core[None]])
        of_key = jnp.where(real, image, -1)[:, None, :]
        member = (
            image[0, :HALF, None] == jnp.arange(IMG_SLOT, dtype=jnp.int32)[None, :]
        ).astype(F32)
        first_cond = noise_cond[:, : 2 * width]
        second_cond = noise_cond[:, 2 * width :]
        head_width = weight_out.shape[0] // 4
        hidden_width = weight_in.shape[1] // 4

        hidden = lax.dynamic_slice(tokens, (core * HALF, 0), (HALF, width)).astype(F32)
        grad_result = lax.dynamic_slice(cotangent, (core * HALF, 0), (HALF, width))
        own = modulate(hidden, member, first_cond).astype(BF)

        early = weight_pieces([weight_query, weight_key, weight_value, weight_out.T])
        *early, own = lax.optimization_barrier((*early, own))
        early_full = along(whole_plane(early, 0, 4 * head_width))
        qkv_full = early_full[:, : 3 * head_width]
        out_full = early_full[:, 3 * head_width :]
        first = gather_rows(own)
        first_mine, shard_in, shard_back = lax.optimization_barrier(
            (first[0], weight_in, weight_back.T)
        )
        first = (first_mine, first[1])
        late = weight_pieces([shard_in, shard_back])
        *late, grad_result = lax.optimization_barrier((*late, grad_result))
        in_full = along(whole_plane(late, 0, hidden_width))
        back_full = along(whole_plane(late, hidden_width, 2 * hidden_width))
        near_grads = jnp.concatenate([grad_result, move(grad_result, near)], axis=0)

        qkv = [nn(rows, qkv_full).astype(BF) for rows in first]
        near_grads, *qkv = lax.optimization_barrier((near_grads, *qkv))
        cotangents = gather_further(near_grads)
        attended = attention(attend_kernel, qkv, slot_facts, of_key, head_width)
        *attended, cot_mine = lax.optimization_barrier((*attended, cotangents[0]))
        cotangents = (cot_mine, cotangents[1])
        middle = hidden + scatter_rows(attended, out_full)
        second = gather_rows(modulate(middle, member, second_cond).astype(BF))
        up = [hidden_up(rows, in_full) for rows in second]
        after = [a for a, _ in up]
        back_part = weight_grad(cotangents, after)
        back_part, *cotangents = lax.optimization_barrier((back_part, *cotangents))
        grad_before = [
            hidden_down(rows, back_full, rate) for rows, (_, rate) in zip(cotangents, up)
        ]
        in_part = weight_grad(second, grad_before)
        in_part, *grad_before = lax.optimization_barrier((in_part, *grad_before))
        grad_second = scatter_rows(grad_before, in_full)

        def norm(rows_in, cond_in):
            return modulate(rows_in, member, cond_in)

        unused, second_pullback = jax.vjp(norm, middle, second_cond)
        grad_middle_norm, grad_second_cond = second_pullback(grad_second)
        grad_middle = grad_result.astype(F32) + grad_middle_norm
        grad_branch = gather_rows(grad_middle.astype(BF))
        grad_attended = [nn(rows, out_full).astype(BF) for rows in grad_branch]
        grad_qkv = attention(
            attend_back_kernel,
            (qkv[0], grad_attended[0], qkv[1], grad_attended[1]),
            slot_facts,
            of_key,
            3 * head_width,
        )
        out_pieces = before_sum(weight_grad(grad_branch, attended))
        qkv_pieces = before_sum(weight_grad(first, grad_qkv))
        blocks = []
        for i in range(3):
            start = i * head_width
            blocks += in_place_order([p[:, start : start + head_width] for p in qkv_pieces])
        last_part = jnp.concatenate(blocks + in_place_order(out_pieces), axis=1)
        last_part, *grad_qkv = lax.optimization_barrier((last_part, *grad_qkv))
        last_part, *after = lax.optimization_barrier((last_part, *after))

        grad_back = along_sum(back_part)
        grad_in = along_sum(in_part)
        grad_last = along_sum(last_part)
        grad_back = after_sum(grad_back)
        *grad_back, grad_in = lax.optimization_barrier((*grad_back, grad_in))
        grad_in = after_sum(grad_in)
        *grad_in, grad_last = lax.optimization_barrier((*grad_in, grad_last))
        grad_back = in_place_order(grad_back)
        grad_in = in_place_order(grad_in)

        grad_first = scatter_rows(grad_qkv, qkv_full)
        result = (middle + scatter_rows(after, back_full)).astype(BF)
        unused, first_pullback = jax.vjp(norm, hidden, first_cond)
        grad_hidden_norm, grad_first_cond = first_pullback(grad_first)
        grad_tokens = grad_middle + grad_hidden_norm
        grad_cond = jnp.concatenate([grad_first_cond, grad_second_cond], axis=1)
        grad_cond = grad_cond + move(grad_cond, sibling)

        def both_halves(rows):
            other = move(rows, sibling)
            low = core == 0
            return jnp.concatenate([jnp.where(low, rows, other), jnp.where(low, other, rows)])

        return (
            both_halves(result),
            both_halves(grad_tokens),
            grad_cond,
            *[grad_last[:, 4 * i * head_width : 4 * (i + 1) * head_width] for i in range(3)],
            grad_last[:, 12 * head_width :].T,
            jnp.concatenate(grad_in, axis=1),
            jnp.concatenate([b.T for b in grad_back], axis=0),
        )

    dp = ("o", "y", "x")
    return jax.shard_map(
        local,
        mesh=inner_mesh,
        in_specs=(
            P(dp, None),
            P(dp, None),
            P(dp),
            P(dp, None),
            P(dp, None),
            P(dp, "mp"),
            P(dp, "mp"),
            P(dp, "mp"),
            P("mp", dp),
            P(dp, "mp"),
            P("mp", dp),
            P(dp, None),
        ),
        out_specs=(
            P(dp, None),
            P(dp, None),
            P(dp, None),
            P(dp, "mp"),
            P(dp, "mp"),
            P(dp, "mp"),
            P("mp", dp),
            P(dp, "mp"),
            P("mp", dp),
        ),
        check_vma=False,
    )
```

```python
import jax
import jax.numpy as jnp
from jax import lax
from jax.experimental import pallas as pl
from jax.experimental.pallas import tpu as pltpu
from jax.sharding import Mesh, PartitionSpec as P

HD = 128
GW = 32
IMG_SLOT = 8
SLOT = 512
HALF = SLOT // 2
EPS = 1e-06
HIGH = lax.Precision.HIGHEST
BF = jnp.bfloat16
F32 = jnp.float32


def arrange(slot_bucket, image_height, image_width, places):
    area_bits = 6 + slot_bucket[:, None]
    across_bits = 3 + ((slot_bucket[:, None] + 1) >> 1)
    image = places[None, :] >> area_bits
    inner = places[None, :] & ((1 << area_bits) - 1)
    grid_row = inner >> across_bits
    grid_col = inner & ((1 << across_bits) - 1)
    real = jnp.zeros(image.shape, bool)
    for i in range(IMG_SLOT):
        tall = image_height[:, i : i + 1]
        broad = image_width[:, i : i + 1]
        real = real | ((image == i) & (grid_row < tall) & (grid_col < broad))
    return image, real


def modulate(hidden, member, cond_part):
    width = hidden.shape[-1]
    mods = jnp.einsum("ti,ic->tc", member, cond_part, precision=HIGH)
    factor = lax.rsqrt(jnp.mean(hidden * hidden, axis=-1, keepdims=True) + EPS)
    return hidden * factor * (1.0 + mods[:, :width]) + mods[:, width:]


def nt(a,b): return lax.dot_general(a,b,(((1,),(1,)),((),())),preferred_element_type=F32)
def nn(a,b): return lax.dot_general(a,b,(((1,),(0,)),((),())),preferred_element_type=F32)
def tn(a,b): return lax.dot_general(a,b,(((0,),(0,)),((),())),preferred_element_type=F32)

def softmax_of(queries, keys_low, allowed):
    scores = nt(queries, keys_low) * HD ** (-0.5)
    scores = jnp.where(allowed, scores, -1e30)
    top = jnp.max(scores, axis=-1, keepdims=True)
    weights = jnp.where(allowed, jnp.exp(scores - top), 0.0)
    return weights / jnp.sum(weights, axis=-1, keepdims=True)

def column(block, i, j, heads):
    at = (i * heads + j) * HD
    return block[:, at : at + HD]

def mask_of(facts, of_key):
    places = lax.broadcasted_iota(jnp.int32, (SLOT, 1), 0) + facts[4]
    image = (places & (SLOT - 1)) >> facts[pl.program_id(0)]
    return image == of_key[0]

def attend_kernel(mine, sib, facts, of_key, out_mine, out_sib):
    allowed = mask_of(facts, of_key)
    rows = jnp.concatenate([mine[...], sib[...]], axis=0)
    heads = rows.shape[1] // (3 * HD)
    made = []
    for j in range(heads):
        probs = softmax_of(column(rows, 0, j, heads), column(rows, 1, j, heads), allowed)
        made.append(nn(probs.astype(BF), column(rows, 2, j, heads)).astype(BF))
    made = jnp.concatenate(made, axis=1)
    out_mine[...] = made[:HALF]
    out_sib[...] = made[HALF:]

def attend_back_kernel(mine, grad_mine, sib, grad_sib, facts, of_key, out_mine, out_sib):
    allowed = mask_of(facts, of_key)
    rows = jnp.concatenate([mine[...], sib[...]], axis=0)
    grads = jnp.concatenate([grad_mine[...], grad_sib[...]], axis=0)
    heads = rows.shape[1] // (3 * HD)
    scale = HD ** (-0.5)
    parts = [[], [], []]
    for j in range(heads):
        queries, keys_low, values = (column(rows, i, j, heads) for i in range(3))
        grad_mixed = column(grads, 0, j, heads)
        probs = softmax_of(queries, keys_low, allowed)
        grad_values = tn(probs.astype(BF), grad_mixed)
        grad_probs = nt(grad_mixed, values)
        grad_scores = probs * (grad_probs - jnp.sum(probs * grad_probs, axis=-1, keepdims=True))
        grad_scores = grad_scores.astype(BF)
        parts[0].append((nn(grad_scores, keys_low) * scale).astype(BF))
        parts[1].append((tn(grad_scores, queries) * scale).astype(BF))
        parts[2].append(grad_values.astype(BF))
    made = jnp.concatenate(parts[0] + parts[1] + parts[2], axis=1)
    out_mine[...] = made[:HALF]
    out_sib[...] = made[HALF:]

def at_mine(s): return (s, 0)
def at_sib(s): return ((s // 2) + (s % 2) * 2, 0)
def at_slot(s): return (s, 0, 0)

def attention(kernel, halves, facts, of_key, width):
    specs = []
    for i, rows in enumerate(halves):
        where = at_mine if i < len(halves) // 2 else at_sib
        specs.append(pl.BlockSpec((HALF, rows.shape[1]), where))
    specs.append(pl.BlockSpec(memory_space=pltpu.SMEM))
    specs.append(pl.BlockSpec((1, 1, SLOT), at_slot))
    made = jax.ShapeDtypeStruct((4 * HALF, width), BF)
    return pl.pallas_call(
        kernel,
        grid=(4,),
        in_specs=specs,
        out_specs=[pl.BlockSpec((HALF, width), at_mine), pl.BlockSpec((HALF, width), at_sib)],
        out_shape=[made, made],
    )(*halves, facts, of_key)

ERFC = (-1.26551223, 1.00002368, 0.37409196, 0.09678418, -0.18628806, 0.27886807,
        -1.13520398, 1.48851587, -0.82215223, 0.17087277)

def gelu_parts(u):
    z = jnp.abs(u) * 0.7071067811865476
    t = 1.0 / (1.0 + 0.5 * z)
    poly = jnp.full_like(t, ERFC[-1])
    for c in ERFC[-2::-1]:
        poly = poly * t + c
    bell = jnp.exp(-0.5 * u * u)
    tail = 0.5 * t * bell * jnp.exp(poly)
    phi = jnp.where(u < 0, tail, 1.0 - tail)
    return u * phi, phi + u * bell * 0.3989422804014327


def up_kernel(rows, weight, after, slope):
    made, rate = gelu_parts(nn(rows[...], weight[...]))
    after[...] = made.astype(BF)
    slope[...] = rate


def down_kernel(rows, weight, slope, grad):
    grad[...] = (nn(rows[...], weight[...]) * slope[...]).astype(BF)


def hidden_up(rows, weight, tile=256):
    count, depth = rows.shape
    width = weight.shape[1]
    by_row = lambda i: (i, 0)
    return pl.pallas_call(
        up_kernel,
        grid=(count // tile,),
        in_specs=[pl.BlockSpec((tile, depth), by_row), pl.BlockSpec((depth, width), lambda i: (0, 0))],
        out_specs=[pl.BlockSpec((tile, width), by_row), pl.BlockSpec((tile, width), by_row)],
        out_shape=[
            jax.ShapeDtypeStruct((count, width), BF),
            jax.ShapeDtypeStruct((count, width), F32),
        ],
    )(rows, weight)


def hidden_down(rows, weight, slope, tile=256):
    count, depth = rows.shape
    width = weight.shape[1]
    by_row = lambda i: (i, 0)
    return pl.pallas_call(
        down_kernel,
        grid=(count // tile,),
        in_specs=[
            pl.BlockSpec((tile, depth), by_row),
            pl.BlockSpec((depth, width), lambda i: (0, 0)),
            pl.BlockSpec((tile, width), by_row),
        ],
        out_specs=pl.BlockSpec((tile, width), by_row),
        out_shape=jax.ShapeDtypeStruct((count, width), BF),
    )(rows, weight, slope)


def grad_kernel(left_mine, right_mine, left_sib, right_sib, made):
    made[...] = tn(left_mine[...], right_mine[...]) + tn(left_sib[...], right_sib[...])


def weight_grad(left, right, tile=512):
    count, depth = left[0].shape
    width = right[0].shape[1]
    specs = [
        pl.BlockSpec((count, tile), lambda i: (0, i)),
        pl.BlockSpec((count, width), lambda i: (0, 0)),
    ]
    return pl.pallas_call(
        grad_kernel,
        grid=(depth // tile,),
        in_specs=specs + specs,
        out_specs=pl.BlockSpec((tile, width), lambda i: (i, 0)),
        out_shape=jax.ShapeDtypeStruct((depth, width), F32),
    )(left[0], right[0], left[1], right[1])


def share(refs, count):
    return refs[0], refs[1 : 1 + count], refs[1 + count :]


def offset(chip, k, step):
    return pl.multiple_of((chip[0] ^ k) * step, step)


def deal_kernel(*refs):
    chip, shards, pieces = share(refs, len(refs) - 5)
    for k, piece in enumerate(pieces):
        at = 0
        for shard in shards:
            part = shard.shape[1] // 4
            piece[:, at : at + part] = shard[:, pl.ds(offset(chip, k, part), part)]
            at += part


def deal(chip, shards):
    rows = shards[0].shape[0]
    width = sum(shard.shape[1] for shard in shards) // 4
    return pl.pallas_call(
        deal_kernel,
        in_specs=[pl.BlockSpec(memory_space=pltpu.SMEM)] + [pl.BlockSpec()] * len(shards),
        out_shape=[jax.ShapeDtypeStruct((rows, width), shards[0].dtype)] * 4,
    )(chip, *shards)


def stack_kernel(*refs):
    chip, pieces, made = share(refs, 4)
    rows = pieces[0].shape[0]
    for k, piece in enumerate(pieces):
        at = 0
        for one in made:
            one[pl.ds(offset(chip, k, rows), rows), :] = piece[:, at : at + one.shape[1]]
            at += one.shape[1]


def stack(chip, pieces, count):
    rows, width = pieces[0].shape
    made = jax.ShapeDtypeStruct((4 * rows, width // count), pieces[0].dtype)
    return pl.pallas_call(
        stack_kernel,
        in_specs=[pl.BlockSpec(memory_space=pltpu.SMEM)] + [pl.BlockSpec()] * 4,
        out_shape=[made] * count,
    )(chip, *pieces)


def align_kernel(*refs):
    chip, pieces, (made,) = share(refs, len(refs) - 2)
    part = pieces[-1].shape[1]
    block = 0
    for first in range(0, len(pieces), 4):
        count = pieces[first].shape[1] // part
        for k in range(4):
            for i in range(count):
                at = pl.ds(4 * (block + i) * part + offset(chip, k, part), part)
                made[:, at] = pieces[first + k][:, i * part : (i + 1) * part]
        block += count


def align(chip, pieces, tile=128):
    rows = pieces[0].shape[0]
    tile = min(tile, rows)
    width = sum(piece.shape[1] for piece in pieces)
    by_row = lambda i: (i, 0)
    return pl.pallas_call(
        align_kernel,
        grid=(rows // tile,),
        in_specs=[pl.BlockSpec(memory_space=pltpu.SMEM)]
        + [pl.BlockSpec((tile, piece.shape[1]), by_row) for piece in pieces],
        out_specs=pl.BlockSpec((tile, width), by_row),
        out_shape=jax.ShapeDtypeStruct((rows, width), pieces[0].dtype),
    )(chip, *pieces)


def grad_pieces_kernel(chip, left_mine, right_mine, left_sib, right_sib, *rest):
    *pieces, made = rest
    made[...] = tn(left_mine[...], right_mine[...]) + tn(left_sib[...], right_sib[...])
    rows = made.shape[0] // 4
    for k, piece in enumerate(pieces):
        piece[...] = made[pl.ds(offset(chip, k, rows), rows), :]


def weight_grad_pieces(chip, left, right, planes):
    count, depth = left[0].shape
    width = right[0].shape[1]
    tile = depth // planes
    specs = [
        pl.BlockSpec((count, tile), lambda i: (0, i)),
        pl.BlockSpec((count, width), lambda i: (0, 0)),
    ]
    return pl.pallas_call(
        grad_pieces_kernel,
        grid=(planes,),
        in_specs=[pl.BlockSpec(memory_space=pltpu.SMEM)] + specs + specs,
        out_specs=[pl.BlockSpec((tile // 4, width), lambda i: (i, 0))] * 4,
        out_shape=[jax.ShapeDtypeStruct((depth // 4, width), F32)] * 4,
        scratch_shapes=[pltpu.VMEM((tile, width), F32)],
    )(chip, left[0], right[0], left[1], right[1])


def solution(mesh):
    outer = mesh.shape["dp"] // 4
    inner_mesh = Mesh(mesh.devices.reshape(outer, 2, 2, 2), ("o", "y", "x", "mp"))
    every = ("o", "y", "x", "mp")

    def pairs(move):
        made = []
        for o in range(outer):
            for y in range(2):
                for x in range(2):
                    for m in range(2):
                        ty, tx, tm = move(y, x, m)
                        made.append(
                            (((o * 2 + y) * 2 + x) * 2 + m, ((o * 2 + ty) * 2 + tx) * 2 + tm)
                        )
        return made

    near = pairs(lambda y, x, m: (y, 1 - x, m) if m == 0 else (1 - y, x, m))
    next_near = pairs(lambda y, x, m: (1 - y, x, m) if m == 0 else (y, 1 - x, m))
    sibling = pairs(lambda y, x, m: (y, x, 1 - m))
    offsets = {
        k: pairs(lambda y, x, m, k=k: (y ^ (k >> 1), x ^ (k & 1), m)) for k in (1, 2, 3)
    }

    def move(value, how):
        return lax.ppermute(value, every, how)

    def gather_rows(own):
        return gather_further(jnp.concatenate([own, move(own, near)], axis=0))

    def gather_further(first):
        mine = jnp.concatenate([first, move(first, next_near)], axis=0)
        return mine, move(mine, sibling)

    def scatter_rows(left, right):
        mine, sib = left
        middle = mine.shape[0] // 2
        far = nt(mine[middle:], right)
        far = far + move(nt(sib[middle:], right).astype(BF), sibling).astype(F32)
        got = move(far.astype(BF), next_near)
        close = nt(mine[:middle], right)
        close = close + move(nt(sib[:middle], right).astype(BF), sibling).astype(F32)
        close = close + got.astype(F32)
        return close[:HALF] + move(close[HALF:].astype(BF), near).astype(F32)

    def exchange(pieces):
        return [pieces[0]] + [move(pieces[k], offsets[k]) for k in (1, 2, 3)]

    def along(value):
        return lax.all_gather(value, "o", axis=0, tiled=True)

    def along_sum(value):
        return lax.psum_scatter(value, "o", scatter_dimension=0, tiled=True)

    def after_sum(mine, chip):
        rows = mine.shape[0] // 4
        return exchange(
            [lax.dynamic_slice_in_dim(mine, (chip[0] ^ k) * rows, rows, 0) for k in range(4)]
        )

    def local(
        tokens,
        noise_cond,
        slot_bucket,
        image_height,
        image_width,
        weight_query,
        weight_key,
        weight_value,
        weight_out,
        weight_in,
        weight_back,
        cotangent,
    ):
        core = lax.axis_index("mp")
        width = tokens.shape[1]
        chip = (lax.axis_index("y") * 2 + lax.axis_index("x"))[None]
        places = (jnp.arange(SLOT, dtype=jnp.int32) + HALF * core) % SLOT
        member = (
            (places[:HALF, None] >> (6 + slot_bucket[0]))
            == jnp.arange(IMG_SLOT, dtype=jnp.int32)[None, :]
        ).astype(F32)
        first_cond = noise_cond[:, : 2 * width]
        second_cond = noise_cond[:, 2 * width :]
        head_width = weight_out.shape[0] // 4

        early = exchange(deal(chip, [weight_query, weight_key, weight_value, weight_out.T]))
        hidden = lax.dynamic_slice(tokens, (core * HALF, 0), (HALF, width)).astype(F32)
        grad_result = lax.dynamic_slice(cotangent, (core * HALF, 0), (HALF, width))
        own = modulate(hidden, member, first_cond).astype(BF)
        facts = jnp.concatenate([slot_bucket[:, None], image_height, image_width], axis=1)
        *early, own, facts = lax.optimization_barrier((*early, own, facts))
        (early_plane,) = stack(chip, early, 1)
        early_plane, own = lax.optimization_barrier((early_plane, own))
        early_full = along(early_plane)
        qkv_full = early_full[:, : 3 * head_width]
        out_full = early_full[:, 3 * head_width :]
        first_near = jnp.concatenate([own, move(own, near)], axis=0)
        late = deal(chip, [weight_in, weight_back.T])
        *late, first_near = lax.optimization_barrier((*late, first_near))
        first = gather_further(first_near)
        late = exchange(late)
        *late, facts = lax.optimization_barrier((*late, facts))
        first_mine, grad_result = lax.optimization_barrier((first[0], grad_result))
        first = (first_mine, first[1])
        in_plane, back_plane = stack(chip, late, 2)
        in_full = along(in_plane)
        back_full = along(back_plane)

        facts = jnp.concatenate([facts, move(facts, near)], axis=0)
        facts = jnp.concatenate([facts, move(facts, next_near)], axis=0)
        image, real = arrange(
            facts[:, 0], facts[:, 1 : 1 + IMG_SLOT], facts[:, 1 + IMG_SLOT :], places
        )
        slot_facts = jnp.concatenate([6 + facts[:, 0], HALF * core[None]])
        of_key = jnp.where(real, image, -1)[:, None, :]
        near_grads = jnp.concatenate([grad_result, move(grad_result, near)], axis=0)

        qkv = [nn(rows, qkv_full).astype(BF) for rows in first]
        attended = attention(attend_kernel, qkv, slot_facts, of_key, head_width)
        *attended, further = lax.optimization_barrier((*attended, move(near_grads, next_near)))
        middle = hidden + scatter_rows(attended, out_full)
        second = gather_rows(modulate(middle, member, second_cond).astype(BF))
        up = [hidden_up(rows, in_full) for rows in second]
        after = [a for a, _ in up]
        cotangents = jnp.concatenate([near_grads, further], axis=0)
        cotangents = (cotangents, move(cotangents, sibling))
        back_part = weight_grad(cotangents, after)
        back_part, *cotangents = lax.optimization_barrier((back_part, *cotangents))
        grad_before = [
            hidden_down(rows, back_full, rate) for rows, (_, rate) in zip(cotangents, up)
        ]
        in_part = weight_grad(second, grad_before)
        in_part, *grad_before = lax.optimization_barrier((in_part, *grad_before))
        grad_second = scatter_rows(grad_before, in_full)

        def norm(rows_in, cond_in):
            return modulate(rows_in, member, cond_in)

        unused, second_pullback = jax.vjp(norm, middle, second_cond)
        grad_middle_norm, grad_second_cond = second_pullback(grad_second)
        grad_middle = grad_result.astype(F32) + grad_middle_norm
        grad_branch = gather_rows(grad_middle.astype(BF))
        grad_attended = [nn(rows, out_full).astype(BF) for rows in grad_branch]
        grad_qkv = attention(
            attend_back_kernel,
            (qkv[0], grad_attended[0], qkv[1], grad_attended[1]),
            slot_facts,
            of_key,
            3 * head_width,
        )
        out_pieces = exchange(weight_grad_pieces(chip, grad_branch, attended, outer))
        qkv_pieces = exchange(weight_grad_pieces(chip, first, grad_qkv, outer))
        last_part = align(chip, qkv_pieces + out_pieces)
        last_part, *grad_qkv = lax.optimization_barrier((last_part, *grad_qkv))
        last_part, *after = lax.optimization_barrier((last_part, *after))

        grad_back = along_sum(back_part)
        grad_in = along_sum(in_part)
        grad_last = along_sum(last_part)
        grad_back = after_sum(grad_back, chip)
        *grad_back, grad_in = lax.optimization_barrier((*grad_back, grad_in))
        grad_in = after_sum(grad_in, chip)
        grad_back = align(chip, grad_back).T
        grad_in = align(chip, grad_in)
        grad_back, grad_in, grad_last = lax.optimization_barrier((grad_back, grad_in, grad_last))

        grad_first = scatter_rows(grad_qkv, qkv_full)
        result = (middle + scatter_rows(after, back_full)).astype(BF)
        unused, first_pullback = jax.vjp(norm, hidden, first_cond)
        grad_hidden_norm, grad_first_cond = first_pullback(grad_first)
        grad_tokens = grad_middle + grad_hidden_norm
        grad_cond = jnp.concatenate([grad_first_cond, grad_second_cond], axis=1)
        grad_cond = grad_cond + move(grad_cond, sibling)

        def both_halves(rows):
            other = move(rows, sibling)
            low = core == 0
            return jnp.concatenate([jnp.where(low, rows, other), jnp.where(low, other, rows)])

        return (
            both_halves(result),
            both_halves(grad_tokens),
            grad_cond,
            *[grad_last[:, 4 * i * head_width : 4 * (i + 1) * head_width] for i in range(3)],
            grad_last[:, 12 * head_width :].T,
            grad_in,
            grad_back,
        )

    dp = ("o", "y", "x")
    return jax.shard_map(
        local,
        mesh=inner_mesh,
        in_specs=(
            P(dp, None),
            P(dp, None),
            P(dp),
            P(dp, None),
            P(dp, None),
            P(dp, "mp"),
            P(dp, "mp"),
            P(dp, "mp"),
            P("mp", dp),
            P(dp, "mp"),
            P("mp", dp),
            P(dp, None),
        ),
        out_specs=(
            P(dp, None),
            P(dp, None),
            P(dp, None),
            P(dp, "mp"),
            P(dp, "mp"),
            P(dp, "mp"),
            P("mp", dp),
            P(dp, "mp"),
            P("mp", dp),
        ),
        check_vma=False,
    )
```

```python
import jax
import jax.numpy as jnp
from jax import lax
from jax.experimental import pallas as pl
from jax.experimental.pallas import tpu as pltpu
from jax.sharding import Mesh, PartitionSpec as P


HD = 128
IMG_SLOT = 8
SLOT = 512
HALF = SLOT // 2
EPS = 1e-06
HIGH = lax.Precision.HIGHEST
BF = jnp.bfloat16
F32 = jnp.float32


def arrange(slot_bucket, image_height, image_width, places):
    area_bits = 6 + slot_bucket[:, None]
    across_bits = 3 + ((slot_bucket[:, None] + 1) >> 1)
    image = places[None, :] >> area_bits
    inner = places[None, :] & ((1 << area_bits) - 1)
    grid_row = inner >> across_bits
    grid_col = inner & ((1 << across_bits) - 1)
    real = jnp.zeros(image.shape, bool)
    for i in range(IMG_SLOT):
        tall = image_height[:, i : i + 1]
        broad = image_width[:, i : i + 1]
        real = real | ((image == i) & (grid_row < tall) & (grid_col < broad))
    return image, real


def modulate(hidden, member, cond_part):
    width = hidden.shape[-1]
    mods = jnp.einsum("ti,ic->tc", member, cond_part, precision=HIGH)
    factor = lax.rsqrt(jnp.mean(hidden * hidden, axis=-1, keepdims=True) + EPS)
    return hidden * factor * (1.0 + mods[:, :width]) + mods[:, width:]


def nt(a,b): return lax.dot_general(a,b,(((1,),(1,)),((),())),preferred_element_type=F32)


def nn(a,b): return lax.dot_general(a,b,(((1,),(0,)),((),())),preferred_element_type=F32)


def tn(a,b): return lax.dot_general(a,b,(((0,),(0,)),((),())),preferred_element_type=F32)


def softmax_of(queries, keys_low, allowed):
    scores = nt(queries, keys_low) * HD ** (-0.5)
    scores = jnp.where(allowed, scores, -1e30)
    top = jnp.max(scores, axis=-1, keepdims=True)
    weights = jnp.where(allowed, jnp.exp(scores - top), 0.0)
    return weights / jnp.sum(weights, axis=-1, keepdims=True)


def column(block, i, j, heads):
    at = (i * heads + j) * HD
    return block[:, at : at + HD]


def mask_of(facts, of_key):
    places = lax.broadcasted_iota(jnp.int32, (SLOT, 1), 0) + facts[4]
    image = (places & (SLOT - 1)) >> facts[pl.program_id(0)]
    return image == of_key[0]


def attend_kernel(mine, sib, facts, of_key, out_mine, out_sib):
    allowed = mask_of(facts, of_key)
    rows = jnp.concatenate([mine[...], sib[...]], axis=0)
    heads = rows.shape[1] // (3 * HD)
    made = []
    for j in range(heads):
        probs = softmax_of(column(rows, 0, j, heads), column(rows, 1, j, heads), allowed)
        made.append(nn(probs.astype(BF), column(rows, 2, j, heads)).astype(BF))
    made = jnp.concatenate(made, axis=1)
    out_mine[...] = made[:HALF]
    out_sib[...] = made[HALF:]


def attend_back_kernel(mine, grad_mine, sib, grad_sib, facts, of_key, out_mine, out_sib):
    allowed = mask_of(facts, of_key)
    rows = jnp.concatenate([mine[...], sib[...]], axis=0)
    grads = jnp.concatenate([grad_mine[...], grad_sib[...]], axis=0)
    heads = rows.shape[1] // (3 * HD)
    scale = HD ** (-0.5)
    parts = [[], [], []]
    for j in range(heads):
        queries, keys_low, values = (column(rows, i, j, heads) for i in range(3))
        grad_mixed = column(grads, 0, j, heads)
        probs = softmax_of(queries, keys_low, allowed)
        grad_values = tn(probs.astype(BF), grad_mixed)
        grad_probs = nt(grad_mixed, values)
        grad_scores = probs * (grad_probs - jnp.sum(probs * grad_probs, axis=-1, keepdims=True))
        grad_scores = grad_scores.astype(BF)
        parts[0].append((nn(grad_scores, keys_low) * scale).astype(BF))
        parts[1].append((tn(grad_scores, queries) * scale).astype(BF))
        parts[2].append(grad_values.astype(BF))
    made = jnp.concatenate(parts[0] + parts[1] + parts[2], axis=1)
    out_mine[...] = made[:HALF]
    out_sib[...] = made[HALF:]


def at_mine(s): return (s, 0)


def at_sib(s): return ((s // 2) + (s % 2) * 2, 0)


def at_slot(s): return (s, 0, 0)


def attention(kernel, halves, facts, of_key, width):
    specs = []
    for i, rows in enumerate(halves):
        where = at_mine if i < len(halves) // 2 else at_sib
        specs.append(pl.BlockSpec((HALF, rows.shape[1]), where))
    specs.append(pl.BlockSpec(memory_space=pltpu.SMEM))
    specs.append(pl.BlockSpec((1, 1, SLOT), at_slot))
    made = jax.ShapeDtypeStruct((4 * HALF, width), BF)
    return pl.pallas_call(
        kernel,
        grid=(4,),
        in_specs=specs,
        out_specs=[pl.BlockSpec((HALF, width), at_mine), pl.BlockSpec((HALF, width), at_sib)],
        out_shape=[made, made],
    )(*halves, facts, of_key)


ERFC = (-1.26551223, 1.00002368, 0.37409196, 0.09678418, -0.18628806, 0.27886807,
        -1.13520398, 1.48851587, -0.82215223, 0.17087277)


def gelu_parts(u):
    z = jnp.abs(u) * 0.7071067811865476
    t = 1.0 / (1.0 + 0.5 * z)
    poly = jnp.full_like(t, ERFC[-1])
    for c in ERFC[-2::-1]:
        poly = poly * t + c
    bell = jnp.exp(-0.5 * u * u)
    tail = 0.5 * t * bell * jnp.exp(poly)
    phi = jnp.where(u < 0, tail, 1.0 - tail)
    return u * phi, phi + u * bell * 0.3989422804014327


def up_kernel(rows, weight, after, slope):
    made, rate = gelu_parts(nn(rows[...], weight[...]))
    after[...] = made.astype(BF)
    slope[...] = rate


def down_kernel(rows, weight, slope, grad):
    grad[...] = (nn(rows[...], weight[...]) * slope[...]).astype(BF)


def hidden_up(rows, weight, tile=256):
    count, depth = rows.shape
    width = weight.shape[1]
    by_row = lambda i: (i, 0)
    return pl.pallas_call(
        up_kernel,
        grid=(count // tile,),
        in_specs=[pl.BlockSpec((tile, depth), by_row), pl.BlockSpec((depth, width), lambda i: (0, 0))],
        out_specs=[pl.BlockSpec((tile, width), by_row), pl.BlockSpec((tile, width), by_row)],
        out_shape=[
            jax.ShapeDtypeStruct((count, width), BF),
            jax.ShapeDtypeStruct((count, width), F32),
        ],
    )(rows, weight)


def hidden_down(rows, weight, slope, tile=256):
    count, depth = rows.shape
    width = weight.shape[1]
    by_row = lambda i: (i, 0)
    return pl.pallas_call(
        down_kernel,
        grid=(count // tile,),
        in_specs=[
            pl.BlockSpec((tile, depth), by_row),
            pl.BlockSpec((depth, width), lambda i: (0, 0)),
            pl.BlockSpec((tile, width), by_row),
        ],
        out_specs=pl.BlockSpec((tile, width), by_row),
        out_shape=jax.ShapeDtypeStruct((count, width), BF),
    )(rows, weight, slope)


def grad_kernel(left_mine, right_mine, left_sib, right_sib, made):
    made[...] = tn(left_mine[...], right_mine[...]) + tn(left_sib[...], right_sib[...])


def half_kernel(where, left_mine, right_mine, left_sib, right_sib, made):
    made[...] = tn(left_mine[...], right_mine[...]) + tn(left_sib[...], right_sib[...])


def weight_grad_half(where, left, right, planes):
    count, depth = left[0].shape
    width = right[0].shape[1]
    tile = depth // planes
    specs = [
        pl.BlockSpec((count, tile), lambda i, at: (0, 2 * i + at[0])),
        pl.BlockSpec((count, width), lambda i, at: (0, 0)),
    ]
    return pl.pallas_call(
        half_kernel,
        grid_spec=pltpu.PrefetchScalarGridSpec(
            num_scalar_prefetch=1,
            grid=(planes // 2,),
            in_specs=specs + specs,
            out_specs=pl.BlockSpec((tile, width), lambda i, at: (i, 0)),
        ),
        out_shape=jax.ShapeDtypeStruct((depth // 2, width), F32),
    )(where, left[0], right[0], left[1], right[1])


def weight_grad(left, right, tile=512):
    count, depth = left[0].shape
    width = right[0].shape[1]
    specs = [
        pl.BlockSpec((count, tile), lambda i: (0, i)),
        pl.BlockSpec((count, width), lambda i: (0, 0)),
    ]
    return pl.pallas_call(
        grad_kernel,
        grid=(depth // tile,),
        in_specs=specs + specs,
        out_specs=pl.BlockSpec((tile, width), lambda i: (i, 0)),
        out_shape=jax.ShapeDtypeStruct((depth, width), F32),
    )(left[0], right[0], left[1], right[1])


def share(refs, count):
    return refs[0], refs[1 : 1 + count], refs[1 + count :]


def offset(chip, k, step):
    return pl.multiple_of((chip[0] ^ k) * step, step)


def deal_kernel(*refs):
    chip, shards, pieces = share(refs, len(refs) - 5)
    for k, piece in enumerate(pieces):
        at = 0
        for shard in shards:
            part = shard.shape[1] // 4
            piece[:, at : at + part] = shard[:, pl.ds(offset(chip, k, part), part)]
            at += part


def deal(chip, shards):
    rows = shards[0].shape[0]
    width = sum(shard.shape[1] for shard in shards) // 4
    return pl.pallas_call(
        deal_kernel,
        in_specs=[pl.BlockSpec(memory_space=pltpu.SMEM)] + [pl.BlockSpec()] * len(shards),
        out_shape=[jax.ShapeDtypeStruct((rows, width), shards[0].dtype)] * 4,
    )(chip, *shards)


def stack_kernel(*refs):
    chip, pieces, made = share(refs, 4)
    rows = pieces[0].shape[0]
    for k, piece in enumerate(pieces):
        at = 0
        for one in made:
            one[pl.ds(offset(chip, k, rows), rows), :] = piece[:, at : at + one.shape[1]]
            at += one.shape[1]


def stack(chip, pieces, count):
    rows, width = pieces[0].shape
    made = jax.ShapeDtypeStruct((4 * rows, width // count), pieces[0].dtype)
    return pl.pallas_call(
        stack_kernel,
        in_specs=[pl.BlockSpec(memory_space=pltpu.SMEM)] + [pl.BlockSpec()] * 4,
        out_shape=[made] * count,
    )(chip, *pieces)


def align_kernel(*refs):
    chip, pieces, (made,) = share(refs, len(refs) - 2)
    part = pieces[-1].shape[1]
    block = 0
    for first in range(0, len(pieces), 4):
        count = pieces[first].shape[1] // part
        for k in range(4):
            for i in range(count):
                at = pl.ds(4 * (block + i) * part + offset(chip, k, part), part)
                made[:, at] = pieces[first + k][:, i * part : (i + 1) * part]
        block += count


def align(chip, pieces, tile=128):
    rows = pieces[0].shape[0]
    tile = min(tile, rows)
    width = sum(piece.shape[1] for piece in pieces)
    by_row = lambda i: (i, 0)
    return pl.pallas_call(
        align_kernel,
        grid=(rows // tile,),
        in_specs=[pl.BlockSpec(memory_space=pltpu.SMEM)]
        + [pl.BlockSpec((tile, piece.shape[1]), by_row) for piece in pieces],
        out_specs=pl.BlockSpec((tile, width), by_row),
        out_shape=jax.ShapeDtypeStruct((rows, width), pieces[0].dtype),
    )(chip, *pieces)


def grad_pieces_kernel(chip, left_mine, right_mine, left_sib, right_sib, *rest):
    *pieces, made = rest
    made[...] = tn(left_mine[...], right_mine[...]) + tn(left_sib[...], right_sib[...])
    rows = made.shape[0] // 4
    for k, piece in enumerate(pieces):
        piece[...] = made[pl.ds(offset(chip, k, rows), rows), :]


def weight_grad_pieces(chip, left, right, planes):
    count, depth = left[0].shape
    width = right[0].shape[1]
    tile = depth // planes
    specs = [
        pl.BlockSpec((count, tile), lambda i: (0, i)),
        pl.BlockSpec((count, width), lambda i: (0, 0)),
    ]
    return pl.pallas_call(
        grad_pieces_kernel,
        grid=(planes,),
        in_specs=[pl.BlockSpec(memory_space=pltpu.SMEM)] + specs + specs,
        out_specs=[pl.BlockSpec((tile // 4, width), lambda i: (i, 0))] * 4,
        out_shape=[jax.ShapeDtypeStruct((depth // 4, width), F32)] * 4,
        scratch_shapes=[pltpu.VMEM((tile, width), F32)],
    )(chip, left[0], right[0], left[1], right[1])


def solution(mesh):
    outer = mesh.shape["dp"] // 4
    inner_mesh = Mesh(mesh.devices.reshape(outer // 2, 2, 2, 2, 2), ("h", "q", "y", "x", "mp"))
    planes = ("h", "q")
    every = ("h", "q", "y", "x", "mp")

    def pairs(move):
        made = []
        for o in range(outer):
            for y in range(2):
                for x in range(2):
                    for m in range(2):
                        ty, tx, tm = move(y, x, m)
                        made.append(
                            (((o * 2 + y) * 2 + x) * 2 + m, ((o * 2 + ty) * 2 + tx) * 2 + tm)
                        )
        return made

    near = pairs(lambda y, x, m: (y, 1 - x, m) if m == 0 else (1 - y, x, m))
    next_near = pairs(lambda y, x, m: (1 - y, x, m) if m == 0 else (y, 1 - x, m))
    sibling = pairs(lambda y, x, m: (y, x, 1 - m))
    offsets = {
        k: pairs(lambda y, x, m, k=k: (y ^ (k >> 1), x ^ (k & 1), m)) for k in (1, 2, 3)
    }

    def planes_apart(step):
        devices = 8 * outer
        return [(d, ((d // 8) ^ step) * 8 + d % 8) for d in range(devices)]

    def move(value, how):
        return lax.ppermute(value, every, how)

    def gather_rows(own):
        return gather_further(jnp.concatenate([own, move(own, near)], axis=0))

    def gather_further(first):
        mine = jnp.concatenate([first, move(first, next_near)], axis=0)
        return mine, move(mine, sibling)

    def scatter_rows(left, right):
        mine, sib = left
        middle = mine.shape[0] // 2
        far = nt(mine[middle:], right)
        far = far + move(nt(sib[middle:], right).astype(BF), sibling).astype(F32)
        got = move(far.astype(BF), next_near)
        close = nt(mine[:middle], right)
        close = close + move(nt(sib[:middle], right).astype(BF), sibling).astype(F32)
        close = close + got.astype(F32)
        return close[:HALF] + move(close[HALF:].astype(BF), near).astype(F32)

    def exchange(pieces):
        return [pieces[0]] + [move(pieces[k], offsets[k]) for k in (1, 2, 3)]

    def along(value):
        return lax.all_gather(value, planes, axis=0, tiled=True)

    def along_sum(value):
        return lax.psum_scatter(value, planes, scatter_dimension=0, tiled=True)

    def sum_planes_last(kept, received):
        if outer != 4:
            return lax.psum_scatter(kept + received, "h", scatter_dimension=0, tiled=True), None
        rows = kept.shape[0] // 2
        mine = lax.axis_index("h")

        def block(i):
            return lax.dynamic_slice_in_dim(kept, i * rows, rows, 0) + (
                lax.dynamic_slice_in_dim(received, i * rows, rows, 0)
            )

        return block(mine), move(block(1 - mine), planes_apart(2))

    def after_sum(mine, chip):
        rows = mine.shape[0] // 4
        return exchange(
            [lax.dynamic_slice_in_dim(mine, (chip[0] ^ k) * rows, rows, 0) for k in range(4)]
        )

    def local(
        tokens,
        noise_cond,
        slot_bucket,
        image_height,
        image_width,
        weight_query,
        weight_key,
        weight_value,
        weight_out,
        weight_in,
        weight_back,
        cotangent,
    ):
        core = lax.axis_index("mp")
        width = tokens.shape[1]
        chip = (lax.axis_index("y") * 2 + lax.axis_index("x"))[None]
        places = (jnp.arange(SLOT, dtype=jnp.int32) + HALF * core) % SLOT
        member = (
            (places[:HALF, None] >> (6 + slot_bucket[0]))
            == jnp.arange(IMG_SLOT, dtype=jnp.int32)[None, :]
        ).astype(F32)
        first_cond = noise_cond[:, : 2 * width]
        second_cond = noise_cond[:, 2 * width :]
        head_width = weight_out.shape[0] // 4

        early = exchange(deal(chip, [weight_query, weight_key, weight_value, weight_out.T]))
        hidden = lax.dynamic_slice(tokens, (core * HALF, 0), (HALF, width)).astype(F32)
        grad_result = lax.dynamic_slice(cotangent, (core * HALF, 0), (HALF, width))
        own = modulate(hidden, member, first_cond).astype(BF)
        facts = jnp.concatenate([slot_bucket[:, None], image_height, image_width], axis=1)
        facts = exchange([facts] * 4)
        *early, own = lax.optimization_barrier((*early, own))
        (early_plane,) = stack(chip, early, 1)
        early_plane, own = lax.optimization_barrier((early_plane, own))
        early_full = along(early_plane)
        qkv_full = early_full[:, : 3 * head_width]
        out_full = early_full[:, 3 * head_width :]
        first_near = jnp.concatenate([own, move(own, near)], axis=0)
        late = deal(chip, [weight_in, weight_back.T])
        *late, first_near = lax.optimization_barrier((*late, first_near))
        first = gather_further(first_near)
        late = exchange(late)
        first_mine, grad_result, *facts = lax.optimization_barrier(
            (first[0], grad_result, *facts)
        )
        first = (first_mine, first[1])
        in_plane, back_plane = stack(chip, late, 2)
        in_full = along(in_plane)
        back_full = along(back_plane)

        low = core == 0
        nearest = jnp.where(low, facts[1], facts[2])
        further = jnp.where(low, facts[2], facts[1])
        facts = jnp.concatenate([facts[0], nearest, further, facts[3]], axis=0)
        image, real = arrange(
            facts[:, 0], facts[:, 1 : 1 + IMG_SLOT], facts[:, 1 + IMG_SLOT :], places
        )
        slot_facts = jnp.concatenate([6 + facts[:, 0], HALF * core[None]])
        of_key = jnp.where(real, image, -1)[:, None, :]
        near_grads = jnp.concatenate([grad_result, move(grad_result, near)], axis=0)

        qkv = [nn(rows, qkv_full).astype(BF) for rows in first]
        attended = attention(attend_kernel, qkv, slot_facts, of_key, head_width)
        *attended, further = lax.optimization_barrier((*attended, move(near_grads, next_near)))
        middle = hidden + scatter_rows(attended, out_full)
        second = gather_rows(modulate(middle, member, second_cond).astype(BF))
        up = [hidden_up(rows, in_full) for rows in second]
        after = [a for a, _ in up]
        cotangents = jnp.concatenate([near_grads, further], axis=0)
        cotangents = (cotangents, move(cotangents, sibling))
        parity = lax.axis_index("q")[None]
        back_sent = weight_grad_half(1 - parity, cotangents, after, outer)
        back_sent, *cotangents = lax.optimization_barrier((back_sent, *cotangents))
        back_got = move(back_sent, planes_apart(1))
        back_kept = weight_grad_half(parity, cotangents, after, outer)
        back_kept, *cotangents = lax.optimization_barrier((back_kept, *cotangents))
        grad_before = [
            hidden_down(rows, back_full, rate) for rows, (_, rate) in zip(cotangents, up)
        ]
        in_part = weight_grad(second, grad_before)
        in_part, *grad_before = lax.optimization_barrier((in_part, *grad_before))
        grad_second = scatter_rows(grad_before, in_full)

        def norm(rows_in, cond_in):
            return modulate(rows_in, member, cond_in)

        unused, second_pullback = jax.vjp(norm, middle, second_cond)
        grad_middle_norm, grad_second_cond = second_pullback(grad_second)
        grad_middle = grad_result.astype(F32) + grad_middle_norm
        grad_branch = gather_rows(grad_middle.astype(BF))
        back_got, *grad_branch = lax.optimization_barrier((back_got, *grad_branch))
        back_mine, back_got = sum_planes_last(back_kept, back_got)
        grad_attended = [nn(rows, out_full).astype(BF) for rows in grad_branch]
        grad_qkv = attention(
            attend_back_kernel,
            (qkv[0], grad_attended[0], qkv[1], grad_attended[1]),
            slot_facts,
            of_key,
            3 * head_width,
        )
        out_pieces = exchange(weight_grad_pieces(chip, grad_branch, attended, outer))
        qkv_pieces = exchange(weight_grad_pieces(chip, first, grad_qkv, outer))
        last_part = align(chip, qkv_pieces + out_pieces)
        last_part, *grad_qkv = lax.optimization_barrier((last_part, *grad_qkv))
        last_part, *after = lax.optimization_barrier((last_part, *after))
        grad_back = back_mine
        if back_got is not None:
            last_part, back_got = lax.optimization_barrier((last_part, back_got))
            grad_back = back_mine + back_got
        grad_in = along_sum(in_part)
        grad_last = along_sum(last_part)
        grad_back = after_sum(grad_back, chip)
        *grad_back, grad_in = lax.optimization_barrier((*grad_back, grad_in))
        grad_in = after_sum(grad_in, chip)
        grad_back = align(chip, grad_back).T
        grad_in = align(chip, grad_in)
        grad_back, grad_in, grad_last = lax.optimization_barrier((grad_back, grad_in, grad_last))

        grad_first = scatter_rows(grad_qkv, qkv_full)
        result = (middle + scatter_rows(after, back_full)).astype(BF)
        unused, first_pullback = jax.vjp(norm, hidden, first_cond)
        grad_hidden_norm, grad_first_cond = first_pullback(grad_first)
        grad_tokens = grad_middle + grad_hidden_norm
        grad_cond = jnp.concatenate([grad_first_cond, grad_second_cond], axis=1)
        grad_cond = grad_cond + move(grad_cond, sibling)

        def both_halves(rows):
            other = move(rows, sibling)
            low = core == 0
            return jnp.concatenate([jnp.where(low, rows, other), jnp.where(low, other, rows)])

        return (
            both_halves(result),
            both_halves(grad_tokens),
            grad_cond,
            *[grad_last[:, 4 * i * head_width : 4 * (i + 1) * head_width] for i in range(3)],
            grad_last[:, 12 * head_width :].T,
            grad_in,
            grad_back,
        )

    dp = ("h", "q", "y", "x")

    return jax.shard_map(
        local,
        mesh=inner_mesh,
        in_specs=(
            P(dp, None),
            P(dp, None),
            P(dp),
            P(dp, None),
            P(dp, None),
            P(dp, "mp"),
            P(dp, "mp"),
            P(dp, "mp"),
            P("mp", dp),
            P(dp, "mp"),
            P("mp", dp),
            P(dp, None),
        ),
        out_specs=(
            P(dp, None),
            P(dp, None),
            P(dp, None),
            P(dp, "mp"),
            P(dp, "mp"),
            P(dp, "mp"),
            P("mp", dp),
            P(dp, "mp"),
            P("mp", dp),
        ),
        check_vma=False,
    )
```

```python
import jax
import jax.numpy as jnp
from jax import lax
from jax.experimental import pallas as pl
from jax.experimental.pallas import tpu as pltpu
from jax.sharding import Mesh, PartitionSpec as P

HD = 128
GW = 32
IMG_SLOT = 8
SLOT = 512
HALF = SLOT // 2
EPS = 1e-06
HIGH = lax.Precision.HIGHEST
BF = jnp.bfloat16
F32 = jnp.float32


def arrange(slot_bucket, image_height, image_width, places):
    area_bits = 6 + slot_bucket[:, None]
    across_bits = 3 + ((slot_bucket[:, None] + 1) >> 1)
    image = places[None, :] >> area_bits
    inner = places[None, :] & ((1 << area_bits) - 1)
    grid_row = inner >> across_bits
    grid_col = inner & ((1 << across_bits) - 1)
    real = jnp.zeros(image.shape, bool)
    for i in range(IMG_SLOT):
        tall = image_height[:, i : i + 1]
        broad = image_width[:, i : i + 1]
        real = real | ((image == i) & (grid_row < tall) & (grid_col < broad))
    return image, real


def modulate(hidden, member, cond_part):
    width = hidden.shape[-1]
    mods = jnp.einsum("ti,ic->tc", member, cond_part, precision=HIGH)
    factor = lax.rsqrt(jnp.mean(hidden * hidden, axis=-1, keepdims=True) + EPS)
    return hidden * factor * (1.0 + mods[:, :width]) + mods[:, width:]


def nt(a,b): return lax.dot_general(a,b,(((1,),(1,)),((),())),preferred_element_type=F32)
def nn(a,b): return lax.dot_general(a,b,(((1,),(0,)),((),())),preferred_element_type=F32)
def tn(a,b): return lax.dot_general(a,b,(((0,),(0,)),((),())),preferred_element_type=F32)

def softmax_of(queries, keys_low, allowed):
    scores = nt(queries, keys_low) * HD ** (-0.5)
    scores = jnp.where(allowed, scores, -1e30)
    top = jnp.max(scores, axis=-1, keepdims=True)
    weights = jnp.where(allowed, jnp.exp(scores - top), 0.0)
    return weights / jnp.sum(weights, axis=-1, keepdims=True)

def column(block, i, j, heads):
    at = (i * heads + j) * HD
    return block[:, at : at + HD]

def mask_of(facts, of_key):
    places = lax.broadcasted_iota(jnp.int32, (SLOT, 1), 0) + facts[4]
    image = (places & (SLOT - 1)) >> facts[pl.program_id(0)]
    return image == of_key[0]

def attend_kernel(mine, sib, facts, of_key, out_mine, out_sib):
    allowed = mask_of(facts, of_key)
    rows = jnp.concatenate([mine[...], sib[...]], axis=0)
    heads = rows.shape[1] // (3 * HD)
    made = []
    for j in range(heads):
        probs = softmax_of(column(rows, 0, j, heads), column(rows, 1, j, heads), allowed)
        made.append(nn(probs.astype(BF), column(rows, 2, j, heads)).astype(BF))
    made = jnp.concatenate(made, axis=1)
    out_mine[...] = made[:HALF]
    out_sib[...] = made[HALF:]

def attend_back_kernel(mine, grad_mine, sib, grad_sib, facts, of_key, out_mine, out_sib):
    allowed = mask_of(facts, of_key)
    rows = jnp.concatenate([mine[...], sib[...]], axis=0)
    grads = jnp.concatenate([grad_mine[...], grad_sib[...]], axis=0)
    heads = rows.shape[1] // (3 * HD)
    scale = HD ** (-0.5)
    parts = [[], [], []]
    for j in range(heads):
        queries, keys_low, values = (column(rows, i, j, heads) for i in range(3))
        grad_mixed = column(grads, 0, j, heads)
        probs = softmax_of(queries, keys_low, allowed)
        grad_values = tn(probs.astype(BF), grad_mixed)
        grad_probs = nt(grad_mixed, values)
        grad_scores = probs * (grad_probs - jnp.sum(probs * grad_probs, axis=-1, keepdims=True))
        grad_scores = grad_scores.astype(BF)
        parts[0].append((nn(grad_scores, keys_low) * scale).astype(BF))
        parts[1].append((tn(grad_scores, queries) * scale).astype(BF))
        parts[2].append(grad_values.astype(BF))
    made = jnp.concatenate(parts[0] + parts[1] + parts[2], axis=1)
    out_mine[...] = made[:HALF]
    out_sib[...] = made[HALF:]

def at_mine(s): return (s, 0)
def at_sib(s): return ((s // 2) + (s % 2) * 2, 0)
def at_slot(s): return (s, 0, 0)

def attention(kernel, halves, facts, of_key, width):
    specs = []
    for i, rows in enumerate(halves):
        where = at_mine if i < len(halves) // 2 else at_sib
        specs.append(pl.BlockSpec((HALF, rows.shape[1]), where))
    specs.append(pl.BlockSpec(memory_space=pltpu.SMEM))
    specs.append(pl.BlockSpec((1, 1, SLOT), at_slot))
    made = jax.ShapeDtypeStruct((4 * HALF, width), BF)
    return pl.pallas_call(
        kernel,
        grid=(4,),
        in_specs=specs,
        out_specs=[pl.BlockSpec((HALF, width), at_mine), pl.BlockSpec((HALF, width), at_sib)],
        out_shape=[made, made],
    )(*halves, facts, of_key)

ERFC = (-1.26551223, 1.00002368, 0.37409196, 0.09678418, -0.18628806, 0.27886807,
        -1.13520398, 1.48851587, -0.82215223, 0.17087277)

def gelu_parts(u):
    z = jnp.abs(u) * 0.7071067811865476
    t = 1.0 / (1.0 + 0.5 * z)
    poly = jnp.full_like(t, ERFC[-1])
    for c in ERFC[-2::-1]:
        poly = poly * t + c
    bell = jnp.exp(-0.5 * u * u)
    tail = 0.5 * t * bell * jnp.exp(poly)
    phi = jnp.where(u < 0, tail, 1.0 - tail)
    return u * phi, phi + u * bell * 0.3989422804014327


def up_kernel(rows, weight, after, slope):
    made, rate = gelu_parts(nn(rows[...], weight[...]))
    after[...] = made.astype(BF)
    slope[...] = rate


def down_kernel(rows, weight, slope, grad):
    grad[...] = (nn(rows[...], weight[...]) * slope[...]).astype(BF)


def hidden_up(rows, weight, tile=256):
    count, depth = rows.shape
    width = weight.shape[1]
    by_row = lambda i: (i, 0)
    return pl.pallas_call(
        up_kernel,
        grid=(count // tile,),
        in_specs=[pl.BlockSpec((tile, depth), by_row), pl.BlockSpec((depth, width), lambda i: (0, 0))],
        out_specs=[pl.BlockSpec((tile, width), by_row), pl.BlockSpec((tile, width), by_row)],
        out_shape=[
            jax.ShapeDtypeStruct((count, width), BF),
            jax.ShapeDtypeStruct((count, width), F32),
        ],
    )(rows, weight)


def hidden_down(rows, weight, slope, tile=256):
    count, depth = rows.shape
    width = weight.shape[1]
    by_row = lambda i: (i, 0)
    return pl.pallas_call(
        down_kernel,
        grid=(count // tile,),
        in_specs=[
            pl.BlockSpec((tile, depth), by_row),
            pl.BlockSpec((depth, width), lambda i: (0, 0)),
            pl.BlockSpec((tile, width), by_row),
        ],
        out_specs=pl.BlockSpec((tile, width), by_row),
        out_shape=jax.ShapeDtypeStruct((count, width), BF),
    )(rows, weight, slope)


def grad_kernel(left_mine, right_mine, left_sib, right_sib, made):
    made[...] = tn(left_mine[...], right_mine[...]) + tn(left_sib[...], right_sib[...])


def weight_grad(left, right, tile=512):
    count, depth = left[0].shape
    width = right[0].shape[1]
    specs = [
        pl.BlockSpec((count, tile), lambda i: (0, i)),
        pl.BlockSpec((count, width), lambda i: (0, 0)),
    ]
    return pl.pallas_call(
        grad_kernel,
        grid=(depth // tile,),
        in_specs=specs + specs,
        out_specs=pl.BlockSpec((tile, width), lambda i: (i, 0)),
        out_shape=jax.ShapeDtypeStruct((depth, width), F32),
    )(left[0], right[0], left[1], right[1])


def share(refs, count):
    return refs[0], refs[1 : 1 + count], refs[1 + count :]


def offset(chip, k, step):
    return pl.multiple_of((chip[0] ^ k) * step, step)


def deal_kernel(*refs):
    chip, shards, pieces = share(refs, len(refs) - 5)
    for k, piece in enumerate(pieces):
        at = 0
        for shard in shards:
            part = shard.shape[1] // 4
            piece[:, at : at + part] = shard[:, pl.ds(offset(chip, k, part), part)]
            at += part


def deal(chip, shards):
    rows = shards[0].shape[0]
    width = sum(shard.shape[1] for shard in shards) // 4
    return pl.pallas_call(
        deal_kernel,
        in_specs=[pl.BlockSpec(memory_space=pltpu.SMEM)] + [pl.BlockSpec()] * len(shards),
        out_shape=[jax.ShapeDtypeStruct((rows, width), shards[0].dtype)] * 4,
    )(chip, *shards)


def stack_kernel(*refs):
    chip, pieces, made = share(refs, 4)
    rows = pieces[0].shape[0]
    for k, piece in enumerate(pieces):
        at = 0
        for one in made:
            one[pl.ds(offset(chip, k, rows), rows), :] = piece[:, at : at + one.shape[1]]
            at += one.shape[1]


def stack(chip, pieces, count):
    rows, width = pieces[0].shape
    made = jax.ShapeDtypeStruct((4 * rows, width // count), pieces[0].dtype)
    return pl.pallas_call(
        stack_kernel,
        in_specs=[pl.BlockSpec(memory_space=pltpu.SMEM)] + [pl.BlockSpec()] * 4,
        out_shape=[made] * count,
    )(chip, *pieces)


def align_kernel(*refs):
    chip, pieces, (made,) = share(refs, len(refs) - 2)
    part = pieces[-1].shape[1]
    block = 0
    for first in range(0, len(pieces), 4):
        count = pieces[first].shape[1] // part
        for k in range(4):
            for i in range(count):
                at = pl.ds(4 * (block + i) * part + offset(chip, k, part), part)
                made[:, at] = pieces[first + k][:, i * part : (i + 1) * part]
        block += count


def align(chip, pieces, tile=128):
    rows = pieces[0].shape[0]
    tile = min(tile, rows)
    width = sum(piece.shape[1] for piece in pieces)
    by_row = lambda i: (i, 0)
    return pl.pallas_call(
        align_kernel,
        grid=(rows // tile,),
        in_specs=[pl.BlockSpec(memory_space=pltpu.SMEM)]
        + [pl.BlockSpec((tile, piece.shape[1]), by_row) for piece in pieces],
        out_specs=pl.BlockSpec((tile, width), by_row),
        out_shape=jax.ShapeDtypeStruct((rows, width), pieces[0].dtype),
    )(chip, *pieces)


def align_turned_kernel(chip, *refs):
    *pieces, made = refs
    for k, piece in enumerate(pieces):
        part = piece.shape[1]
        made[pl.ds(offset(chip, k, part), part), :] = piece[...].T


def align_turned(chip, pieces):
    rows, part = pieces[0].shape
    return pl.pallas_call(
        align_turned_kernel,
        in_specs=[pl.BlockSpec(memory_space=pltpu.SMEM)] + [pl.BlockSpec()] * 4,
        out_shape=jax.ShapeDtypeStruct((4 * part, rows), pieces[0].dtype),
    )(chip, *pieces)


def grad_pieces_kernel(chip, left_mine, right_mine, left_sib, right_sib, *rest):
    *pieces, made = rest
    made[...] = tn(left_mine[...], right_mine[...]) + tn(left_sib[...], right_sib[...])
    rows = made.shape[0] // 4
    for k, piece in enumerate(pieces):
        piece[...] = made[pl.ds(offset(chip, k, rows), rows), :]


def weight_grad_pieces(chip, left, right, planes):
    count, depth = left[0].shape
    width = right[0].shape[1]
    tile = depth // planes
    specs = [
        pl.BlockSpec((count, tile), lambda i: (0, i)),
        pl.BlockSpec((count, width), lambda i: (0, 0)),
    ]
    return pl.pallas_call(
        grad_pieces_kernel,
        grid=(planes,),
        in_specs=[pl.BlockSpec(memory_space=pltpu.SMEM)] + specs + specs,
        out_specs=[pl.BlockSpec((tile // 4, width), lambda i: (i, 0))] * 4,
        out_shape=[jax.ShapeDtypeStruct((depth // 4, width), F32)] * 4,
        scratch_shapes=[pltpu.VMEM((tile, width), F32)],
    )(chip, left[0], right[0], left[1], right[1])


def solution(mesh):
    outer = mesh.shape["dp"] // 4
    inner_mesh = Mesh(mesh.devices.reshape(outer, 2, 2, 2), ("o", "y", "x", "mp"))
    every = ("o", "y", "x", "mp")

    def pairs(move):
        made = []
        for o in range(outer):
            for y in range(2):
                for x in range(2):
                    for m in range(2):
                        ty, tx, tm = move(y, x, m)
                        made.append(
                            (((o * 2 + y) * 2 + x) * 2 + m, ((o * 2 + ty) * 2 + tx) * 2 + tm)
                        )
        return made

    near = pairs(lambda y, x, m: (y, 1 - x, m) if m == 0 else (1 - y, x, m))
    next_near = pairs(lambda y, x, m: (1 - y, x, m) if m == 0 else (y, 1 - x, m))
    sibling = pairs(lambda y, x, m: (y, x, 1 - m))
    offsets = {
        k: pairs(lambda y, x, m, k=k: (y ^ (k >> 1), x ^ (k & 1), m)) for k in (1, 2, 3)
    }

    def move(value, how):
        return lax.ppermute(value, every, how)

    def gather_rows(own):
        return gather_further(jnp.concatenate([own, move(own, near)], axis=0))

    def gather_further(first):
        mine = jnp.concatenate([first, move(first, next_near)], axis=0)
        return mine, move(mine, sibling)

    def scatter_rows(left, right):
        mine, sib = left
        middle = mine.shape[0] // 2
        far = nt(mine[middle:], right)
        far = far + move(nt(sib[middle:], right).astype(BF), sibling).astype(F32)
        got = move(far.astype(BF), next_near)
        close = nt(mine[:middle], right)
        close = close + move(nt(sib[:middle], right).astype(BF), sibling).astype(F32)
        close = close + got.astype(F32)
        return close[:HALF] + move(close[HALF:].astype(BF), near).astype(F32)

    def exchange(pieces):
        return [pieces[0]] + [move(pieces[k], offsets[k]) for k in (1, 2, 3)]

    def along(value):
        return lax.all_gather(value, "o", axis=0, tiled=True)

    def along_sum(value):
        return lax.psum_scatter(value, "o", scatter_dimension=0, tiled=True)

    def after_sum(mine, chip):
        rows = mine.shape[0] // 4
        return exchange(
            [lax.dynamic_slice_in_dim(mine, (chip[0] ^ k) * rows, rows, 0) for k in range(4)]
        )

    def local(
        tokens,
        noise_cond,
        slot_bucket,
        image_height,
        image_width,
        weight_query,
        weight_key,
        weight_value,
        weight_out,
        weight_in,
        weight_back,
        cotangent,
    ):
        core = lax.axis_index("mp")
        width = tokens.shape[1]
        chip = (lax.axis_index("y") * 2 + lax.axis_index("x"))[None]
        places = (jnp.arange(SLOT, dtype=jnp.int32) + HALF * core) % SLOT
        member = (
            (places[:HALF, None] >> (6 + slot_bucket[0]))
            == jnp.arange(IMG_SLOT, dtype=jnp.int32)[None, :]
        ).astype(F32)
        first_cond = noise_cond[:, : 2 * width]
        second_cond = noise_cond[:, 2 * width :]
        head_width = weight_out.shape[0] // 4

        early = exchange(deal(chip, [weight_query, weight_key, weight_value, weight_out.T]))
        hidden = lax.dynamic_slice(tokens, (core * HALF, 0), (HALF, width)).astype(F32)
        grad_result = lax.dynamic_slice(cotangent, (core * HALF, 0), (HALF, width))
        own = modulate(hidden, member, first_cond).astype(BF)
        facts = jnp.concatenate([slot_bucket[:, None], image_height, image_width], axis=1)
        *early, own = lax.optimization_barrier((*early, own))
        (early_plane,) = stack(chip, early, 1)
        early_plane, own = lax.optimization_barrier((early_plane, own))
        early_full = along(early_plane)
        qkv_full = early_full[:, : 3 * head_width]
        out_full = early_full[:, 3 * head_width :]
        first_near = jnp.concatenate([own, move(own, near)], axis=0)
        first = gather_further(first_near)
        late = deal(chip, [weight_in, weight_back.T])
        first_mine, *late = lax.optimization_barrier((first[0], *late))
        first = (first_mine, first[1])
        late = exchange(late)
        *late, grad_result, facts = lax.optimization_barrier((*late, grad_result, facts))
        facts = exchange([facts] * 4)
        in_plane, back_plane = stack(chip, late, 2)
        in_full = along(in_plane)
        back_full = along(back_plane)

        low = core == 0
        nearest = jnp.where(low, facts[1], facts[2])
        further = jnp.where(low, facts[2], facts[1])
        facts = jnp.concatenate([facts[0], nearest, further, facts[3]], axis=0)
        image, real = arrange(
            facts[:, 0], facts[:, 1 : 1 + IMG_SLOT], facts[:, 1 + IMG_SLOT :], places
        )
        slot_facts = jnp.concatenate([6 + facts[:, 0], HALF * core[None]])
        of_key = jnp.where(real, image, -1)[:, None, :]
        near_grads = jnp.concatenate([grad_result, move(grad_result, near)], axis=0)

        qkv = [nn(rows, qkv_full).astype(BF) for rows in first]
        attended = attention(attend_kernel, qkv, slot_facts, of_key, head_width)
        *attended, further = lax.optimization_barrier((*attended, move(near_grads, next_near)))
        middle = hidden + scatter_rows(attended, out_full)
        cot_mine = jnp.concatenate([near_grads, further], axis=0)
        middle, cot_mine = lax.optimization_barrier((middle, cot_mine))
        second = gather_rows(modulate(middle, member, second_cond).astype(BF))
        up = [hidden_up(rows, in_full) for rows in second]
        after = [a for a, _ in up]
        cotangents = (cot_mine, move(cot_mine, sibling))
        back_part = weight_grad(cotangents, after)
        back_part, *cotangents = lax.optimization_barrier((back_part, *cotangents))
        grad_before = [
            hidden_down(rows, back_full, rate) for rows, (_, rate) in zip(cotangents, up)
        ]
        in_part = weight_grad(second, grad_before)
        in_part, *grad_before = lax.optimization_barrier((in_part, *grad_before))
        grad_second = scatter_rows(grad_before, in_full)

        def norm(rows_in, cond_in):
            return modulate(rows_in, member, cond_in)

        unused, second_pullback = jax.vjp(norm, middle, second_cond)
        grad_middle_norm, grad_second_cond = second_pullback(grad_second)
        grad_middle = grad_result.astype(F32) + grad_middle_norm
        grad_branch = gather_rows(grad_middle.astype(BF))
        grad_attended = [nn(rows, out_full).astype(BF) for rows in grad_branch]
        grad_qkv = attention(
            attend_back_kernel,
            (qkv[0], grad_attended[0], qkv[1], grad_attended[1]),
            slot_facts,
            of_key,
            3 * head_width,
        )
        out_pieces = exchange(weight_grad_pieces(chip, grad_branch, attended, outer))
        qkv_pieces = exchange(weight_grad_pieces(chip, first, grad_qkv, outer))
        last_part = align(chip, qkv_pieces + out_pieces)
        last_part, *grad_qkv = lax.optimization_barrier((last_part, *grad_qkv))
        last_part, *after = lax.optimization_barrier((last_part, *after))

        grad_back = along_sum(back_part)
        grad_in = along_sum(in_part)
        grad_last = along_sum(last_part)
        grad_back = after_sum(grad_back, chip)
        *grad_back, grad_in = lax.optimization_barrier((*grad_back, grad_in))
        grad_in = after_sum(grad_in, chip)
        grad_back = align_turned(chip, grad_back)
        grad_in = align(chip, grad_in)
        grad_back, grad_in, grad_last = lax.optimization_barrier((grad_back, grad_in, grad_last))

        grad_first = scatter_rows(grad_qkv, qkv_full)
        result = (middle + scatter_rows(after, back_full)).astype(BF)
        unused, first_pullback = jax.vjp(norm, hidden, first_cond)
        grad_hidden_norm, grad_first_cond = first_pullback(grad_first)
        grad_tokens = grad_middle + grad_hidden_norm
        grad_cond = jnp.concatenate([grad_first_cond, grad_second_cond], axis=1)
        grad_cond = grad_cond + move(grad_cond, sibling)

        def both_halves(rows):
            other = move(rows, sibling)
            low = core == 0
            return jnp.concatenate([jnp.where(low, rows, other), jnp.where(low, other, rows)])

        return (
            both_halves(result),
            both_halves(grad_tokens),
            grad_cond,
            *[grad_last[:, 4 * i * head_width : 4 * (i + 1) * head_width] for i in range(3)],
            grad_last[:, 12 * head_width :].T,
            grad_in,
            grad_back,
        )

    dp = ("o", "y", "x")
    return jax.shard_map(
        local,
        mesh=inner_mesh,
        in_specs=(
            P(dp, None),
            P(dp, None),
            P(dp),
            P(dp, None),
            P(dp, None),
            P(dp, "mp"),
            P(dp, "mp"),
            P(dp, "mp"),
            P("mp", dp),
            P(dp, "mp"),
            P("mp", dp),
            P(dp, None),
        ),
        out_specs=(
            P(dp, None),
            P(dp, None),
            P(dp, None),
            P(dp, "mp"),
            P(dp, "mp"),
            P(dp, "mp"),
            P("mp", dp),
            P(dp, "mp"),
            P("mp", dp),
        ),
        check_vma=False,
    )
```
